32 devices in a mesh: sect: 2 (over core), row: 2 (over y), col: 8 (over z, x).
Axes of the slice: x: 2, y: 2, z: 4, core: 2. Of those that a mesh axis runs over, the one named last changes fastest.
Arguments:
- log_trans: float32 [256, 1024], P('row', 'col'), may hold values from -3 to 3
- corr_len: float32 [2], replicated, may hold values from 1.5 to 3
- taper_width: int32 [2], replicated, may hold values from 1 to 4, as said below
- well_cells: int32 [2, 8], replicated, may hold values from 0 to 262143
- obs_weight: bfloat16 [2, 8, 256, 1024], P('sect', None, 'row', 'col'), may hold values from -0.0048828125 to 0.0048828125
Outputs:
- qh_fields: bfloat16 [2, 8, 256, 1024], P('sect', None, 'row', 'col')
- measure_cov: float32 [16, 16], replicated
The draws below stay inside these ranges and needn't reach their ends.
Inputs may be any that keep to these rules, and one draw needn't show every extreme that they name: `taper_width`: one of the two widths equals 4.
All inputs are finite; a program needn't handle non-finite values.
Results may differ from the reference program's by a relative error of at most 0.0041.
Values may be sent and summed in bfloat16 or wider, within the bound.
No kernel may reach another device: no remote copies, remote signals or barrier semaphores. Data moves between devices by JAX's collectives and lax.ppermute only.
A program may use at most 64 MiB of HBM per device.

```python
import math
import jax
import jax.numpy as jnp
from jax import lax

BLOCK = 128
TAPER = 4
SWEEPS = 24
WELLS = 8
BATCHES = 2
NR = 256
NC = 1024


def draw_taper_width(key, part):
    first_key, second_key = jax.random.split(key)
    other_width = jax.random.randint(first_key, (), 1, TAPER + 1)
    which_side = jax.random.randint(second_key, (), 0, 2)
    return jnp.where(jnp.arange(2) == which_side, TAPER, other_width).astype(jnp.int32)


def set_ends(drawn, key, low, largest):
    place = [jax.random.randint(jax.random.fold_in(key, axis), (), 0, length) for axis, length in enumerate(drawn.shape)]
    widest = drawn.shape.index(max(drawn.shape))
    next_to = place[:widest] + [(place[widest] + 1) % drawn.shape[widest]] + place[widest + 1:]
    return drawn.at[tuple(place)].set(low).at[tuple(next_to)].set(largest)


def block_levels(stream_key, shape, pieces, smallest, top_value):
    level, own = 1.0, jax.random.fold_in(stream_key, 6)
    for dim, shards_of in pieces:
        steps = jnp.exp(jax.random.uniform(jax.random.fold_in(own, dim), (shards_of,), jnp.float32, smallest / len(pieces), top_value / len(pieces)))
        level = level * jnp.repeat(steps, shape[dim] // shards_of).reshape([-1 if axis == dim else 1 for axis in range(len(shape))])
    return level


def scatter_about(rng, shape, scale, reach, shards=(), kind=jnp.bfloat16):
    values = jax.random.normal(rng, shape, jnp.float32) * scale
    if len(shards) > 0:
        values = block_levels(rng, shape, shards, -0.22, 0.18) * values
    return jnp.clip(values, min=-reach, max=reach).astype(kind)


def setup_inputs(seed: int = 0) -> dict:
    arg_keys = jax.random.split(jax.random.key(seed), 6)
    return {
        "log_trans": scatter_about(arg_keys[0], (NR, NC), 0.7, 3.0, ((0, 2), (1, 8)), jnp.float32),
        "corr_len": jnp.clip(jnp.exp(jax.random.uniform(arg_keys[1], (2,), jnp.float32, math.log(1.5), math.log(3.0))), 1.5, 3.0),
        "taper_width": draw_taper_width(jax.random.fold_in(arg_keys[5], 71), 0),
        "well_cells": set_ends(jax.random.randint(arg_keys[3], (BATCHES, WELLS), 0, NR * NC), jax.random.fold_in(arg_keys[3], 1), 0, (NR * NC) - 1).astype(jnp.int32),
        "obs_weight": scatter_about(arg_keys[4], (BATCHES, WELLS, NR, NC), (1.0 / (10 * BLOCK)), 0.0048828125, ((0, 2), (2, 2), (3, 8))),
    }


leakage = 0.05


def harmonic(left_value, right_value):
    return 2.0 * left_value * right_value / (left_value + right_value)


def face_terms(log_trans):
    conductance = jnp.exp(log_trans)
    east_face = jnp.concatenate([harmonic(conductance[:, :-1], conductance[:, 1:]), conductance[:, -1:]], axis=1)
    west_face = jnp.concatenate([conductance[:, :1], harmonic(conductance[:, 1:], conductance[:, :-1])], axis=1)
    north_face = jnp.concatenate([conductance[:1], harmonic(conductance[1:], conductance[:-1])], axis=0)
    south_face = jnp.concatenate([harmonic(conductance[:-1], conductance[1:]), conductance[-1:]], axis=0)
    diagonal_sum = east_face + west_face + north_face + south_face + leakage
    return east_face, west_face, north_face, south_face, diagonal_sum


def jacobi_sweep(current, source, faces):
    east_face, west_face, north_face, south_face, diagonal_sum = faces
    padded = jnp.pad(current, ((0, 0), (1, 1), (1, 1)))
    summed = source + east_face * padded[:, 1:-1, 2:] + west_face * padded[:, 1:-1, :-2]
    summed = summed + north_face * padded[:, :-2, 1:-1] + south_face * padded[:, 2:, 1:-1]
    return summed / diagonal_sum


def band_matrix(extent, corr_scale, taper_reach):
    position = jnp.arange(extent, dtype=jnp.int32)
    distance = jnp.abs(position[:, None] - position[None, :]).astype(jnp.float32)
    return (jnp.exp(-distance / corr_scale) * jnp.maximum(1.0 - distance / taper_reach, 0.0)).astype(jnp.bfloat16)


def reference(log_trans, corr_len, taper_width, well_cells, obs_weight):
    faces = face_terms(log_trans)
    row_scale = corr_len[0] * (NR / 4.0)
    row_reach = (taper_width[0] + TAPER).astype(jnp.float32) * (NR / (2.0 * TAPER)) + 1.0
    col_scale = corr_len[1] * BLOCK
    col_reach = (taper_width[1] * BLOCK + 1).astype(jnp.float32)
    row_band = band_matrix(NR, row_scale, row_reach)
    col_band = band_matrix(NC, col_scale, col_reach)

    def one_batch(batch_weight):
        source = batch_weight.astype(jnp.float32)
        state = lax.fori_loop(0, SWEEPS, lambda sweep_index, current: jacobi_sweep(current, source, faces),
                              jnp.zeros((WELLS, NR, NC), jnp.float32))
        adjoint = state.astype(jnp.bfloat16)
        mixed = jnp.dot(adjoint.reshape(WELLS * NR, NC), col_band, preferred_element_type=jnp.float32)
        mixed = mixed.astype(jnp.bfloat16).reshape(WELLS, NR, NC)
        return lax.map(lambda well_plane: jnp.dot(row_band, well_plane, preferred_element_type=jnp.float32).astype(jnp.bfloat16), mixed)

    qh_fields = lax.map(one_batch, obs_weight)
    flattened = qh_fields.reshape(BATCHES * WELLS, NR * NC)
    sampled = jnp.take(flattened, well_cells.reshape(-1), axis=1).astype(jnp.float32)
    return qh_fields, jnp.transpose(sampled)
```

```python
import functools

import jax
import jax.numpy as jnp
from jax import lax
from jax.experimental import pallas as pl
from jax.experimental.pallas import tpu as pltpu
from jax.sharding import PartitionSpec as P

BLOCK = 128
TAPER = 4
SWEEPS = 24
HALO = 24
LANES = 128
STRIP = 32

leakage = 0.05
F32, BF16 = jnp.float32, jnp.bfloat16


def iota(shape, dim):
    return lax.broadcasted_iota(jnp.int32, shape, dim)


def one_hot(mask):
    return jnp.where(mask, 1.0, 0.0).astype(BF16)


def dot(a, b):
    return jnp.dot(a, b, preferred_element_type=F32)


def harmonic(a, b):
    return 2.0 * a * b / (a + b)


def factor(offset, scale, reach):
    distance = jnp.abs(offset).astype(F32)
    return jnp.exp(-distance / scale) * jnp.maximum(1.0 - distance / reach, 0.0)


def scales(corr_ref, taper_ref, total_rows):
    row_scale = corr_ref[0] * (total_rows / 4.0)
    row_reach = (taper_ref[0] + TAPER).astype(F32) * (total_rows / (2.0 * TAPER)) + 1.0
    col_scale = corr_ref[1] * BLOCK
    col_reach = (taper_ref[1] * BLOCK + 1).astype(F32)
    return row_scale, row_reach, col_scale, col_reach


def pack_kernel(swapped, place_ref, *refs):
    if swapped:
        obs_ref, recv_ref, lt_ref, lt_recv_ref, full_ref, split_ref, a_ref, b_ref = refs
    else:
        obs_ref, lt_ref, full_ref, split_ref, a_ref, b_ref = refs
    wells, rows, _ = full_ref.shape
    if swapped:
        half = rows // 2
        mine = pl.multiple_of(place_ref[0] * half, half)
        other = pl.multiple_of(half - mine, half)
        first = place_ref[0] * wells
        for w in range(wells):
            full_ref[w, pl.ds(mine, half), :] = obs_ref[first + w]
            full_ref[w, pl.ds(other, half), :] = recv_ref[w]
        parts = [(lt_ref[...], pl.ds(mine, half)), (lt_recv_ref[...], pl.ds(other, half))]
    else:
        full_ref[...] = obs_ref[...]
        parts = [(lt_ref[...], pl.ds(0, rows))]
    for value, where in parts:
        for i in range(3):
            piece = value.astype(BF16)
            split_ref[i, where, :] = piece
            value = value - piece.astype(F32)
    even = lax.rem(place_ref[1], 2) == 0
    src, dst = iota((LANES, LANES), 0), iota((LANES, LANES), 1)
    tail = LANES - HALO
    start_a = jnp.where(even, tail, 0)
    for out_ref, start in ((a_ref, start_a), (b_ref, tail - start_a)):
        for group, (ref, count) in enumerate(((full_ref, wells), (split_ref, 3))):
            total = jnp.zeros((rows, LANES), F32)
            for i in range(count):
                k = dst - STRIP * i
                pick = one_hot((src == k + start) & (k >= 0) & (k < HALO))
                total = total + dot(ref[i], pick)
            out_ref[:, group * LANES : (group + 1) * LANES] = total.astype(BF16)


def pair_swap(value, wells, outer):
    groups = 8 // wells
    group = iota(value.shape, 0) // wells
    up = pltpu.roll(value, wells, 0)
    if groups == 2:
        return up
    down = pltpu.roll(value, 8 - wells, 0)
    return jnp.where((group % 2 == 0) == (not outer), down, up)


def update(previous, current, following, coefs, source):
    result = []
    even, odd = current
    sides = ((odd, pltpu.roll(odd, 1, 1)), (pltpu.roll(even, LANES - 1, 1), even))
    for p in range(2):
        ce, cw, co, ci = coefs[4 * p : 4 * p + 4]
        east, west = sides[p]
        result.append(
            (source[p] + ce * east) + (cw * west + co * previous[p]) + ci * following[p]
        )
    return result


def sweep_kernel(total_cols, place_ref, corr_ref, taper_ref, cells_ref,
                 full_ref, split_ref, a_ref, b_ref, adj_ref, mom_ref,
                 nat_ref, x_ref, s_ref, c_ref):
    wells, rows, _ = full_ref.shape
    groups = 8 // wells
    seg = rows // groups
    col = place_ref[1]
    even = lax.rem(col, 2) == 0
    src, dst = iota((LANES, 2 * LANES), 0), iota((LANES, 2 * LANES), 1)
    window = 2 * (dst % LANES) + dst // LANES
    own_pick = one_hot(window == src + HALO)
    right = LANES + HALO
    base_a = jnp.where(even, right, 0)
    picks = []
    for i in range(max(wells, 3)):
        k = src - STRIP * i
        live = (k >= 0) & (k < HALO)
        picks.append(tuple(
            one_hot((window == k + base) & live) for base in (base_a, right - base_a)
        ))

    def widened(ref, i, group):
        lanes = slice(group * LANES, (group + 1) * LANES)
        return (
            dot(ref[i], own_pick)
            + dot(a_ref[:, lanes], picks[i][0])
            + dot(b_ref[:, lanes], picks[i][1])
        )

    planes = [widened(split_ref, i, 1) for i in range(3)]
    nat_ref[0:8, :] = jnp.zeros((8, 2 * LANES), F32)
    nat_ref[rows + 8 : rows + 16, :] = jnp.zeros((8, 2 * LANES), F32)
    nat_ref[8 : rows + 8, :] = planes[0] + planes[1] + planes[2]
    planes = [plane.astype(BF16) for plane in planes]
    fields = [widened(full_ref, w, 0) for w in range(wells)]

    lane = iota((seg, LANES), 1)
    step = iota((seg, LANES), 0)
    t_pick, r_pick = iota((seg + 16, rows), 0), iota((seg + 16, rows), 1)
    t_flip, r_flip = iota((seg, rows), 0), iota((seg, rows), 1)
    for g in range(groups):
        if g % 2 == 0:
            logs = nat_ref[g * seg : g * seg + seg + 16, :]
        else:
            pick = one_hot(r_pick == (g + 1) * seg - 1 - (t_pick - 8))
            logs = dot(pick, planes[0]) + dot(pick, planes[1]) + dot(pick, planes[2])
            flip = one_hot(r_flip == (g + 1) * seg - 1 - t_flip)
        cond = jnp.exp(logs)
        sides = [cond[:, :LANES], cond[:, LANES:]]
        centre = [side[8 : seg + 8] for side in sides]
        east = (centre[1], pltpu.roll(centre[0], LANES - 1, 1))
        west = (pltpu.roll(centre[1], 1, 1), centre[0])
        edge = (step == 0) if g in (0, groups - 1) else None
        inverse = []
        for p in range(2):
            column = col * LANES - HALO + 2 * lane + p
            inside = (column >= 0) & (column < total_cols) & (lane < (LANES + 2 * HALO) // 2)
            has_east, has_west = column < total_cols - 1, column > 0
            mid = centre[p]
            fe = jnp.where(has_east, harmonic(mid, east[p]), mid)
            fw = jnp.where(has_west, harmonic(mid, west[p]), mid)
            fo = harmonic(mid, sides[p][7 : seg + 7])
            if edge is not None:
                fo = jnp.where(edge, mid, fo)
            fi = harmonic(mid, sides[p][9 : seg + 9])
            inv = jnp.where(inside, 1.0 / (fe + fw + fo + fi + leakage), 0.0)
            inverse.append(inv)
            outer = fo * inv
            if edge is not None:
                outer = jnp.where(edge, 0.0, outer)
            coefs = (
                jnp.where(has_east, fe * inv, 0.0),
                jnp.where(has_west, fw * inv, 0.0),
                outer,
                fi * inv,
            )
            for d, coef in enumerate(coefs):
                for t in range(0, seg, 8):
                    for w in range(wells):
                        at = ((t * 2 + p) * 4 + d) * 8 + g * wells + w
                        c_ref[pl.ds(at, 8, stride=64), :] = coef[t : t + 8]
        for w in range(wells):
            if g % 2 == 0:
                field = fields[w][g * seg : (g + 1) * seg]
            else:
                field = dot(flip, fields[w].astype(BF16))
            for p in range(2):
                value = field[:, p * LANES : (p + 1) * LANES] * inverse[p]
                for t in range(0, seg, 8):
                    at = (t * 2 + p) * 8 + g * wells + w
                    s_ref[pl.ds(at, 8, stride=16), :] = value[t : t + 8]

    def load(ref, t, count=2):
        at = pl.multiple_of(t * (count * 8), count * 8)
        return [ref[pl.ds(at + 8 * i, 8), :] for i in range(count)]

    def save(t, value):
        at = pl.multiple_of(t * 16, 16)
        for p in range(2):
            x_ref[pl.ds(at + 8 * p, 8), :] = value[p]

    unroll = 8

    def march(first_pass):
        def rows_of(t0, carry, first_block):
            x0, x1, y0, y1, coefs1, source1 = carry
            for i in range(unroll):
                t = t0 + i
                coefs2 = load(c_ref, t, 8)
                source2 = load(s_ref, t)
                if first_pass:
                    y2 = source2
                else:
                    x2 = load(x_ref, t + 2)
                    y2 = update(x0, x1, x2, coefs2, source2)
                    x0, x1 = x1, x2
                if first_block and i == 0:
                    y0 = [pair_swap(v, wells, True) for v in y2]
                    y0, y1 = y0, y2
                else:
                    save(t, update(y0, y1, y2, coefs1, source1))
                    y0, y1 = y1, y2
                coefs1, source1 = coefs2, source2
            return x0, x1, y0, y1, coefs1, source1

        blank = [jnp.zeros((8, LANES), F32)] * 2
        if first_pass:
            x0 = x1 = blank
        else:
            x1 = load(x_ref, 1)
            x0 = [pair_swap(v, wells, True) for v in x1]
            last = load(x_ref, seg)
            save(seg + 1, [pair_swap(v, wells, False) for v in last])
        carry = rows_of(0, (x0, x1, blank, blank, None, None), True)
        carry = lax.fori_loop(
            1, seg // unroll, lambda b, c: rows_of(b * unroll, c, False), carry
        )
        _, _, y0, y1, coefs1, source1 = carry
        y2 = [pair_swap(v, wells, False) for v in y1]
        save(seg, update(y0, y1, y2, coefs1, source1))

    march(True)

    def more(_, carry):
        march(False)
        return carry

    lax.fori_loop(0, SWEEPS // 2 - 1, more, 0)

    row_scale, row_reach, col_scale, col_reach = scales(corr_ref, taper_ref, rows)
    order = one_hot(
        2 * (iota((2 * LANES, LANES), 0) % LANES) + iota((2 * LANES, LANES), 0) // LANES
        == iota((2 * LANES, LANES), 1) + HALO
    )
    reverse = one_hot(iota((seg, seg), 0) == seg - 1 - iota((seg, seg), 1))
    kind, c = iota((8, LANES), 0), iota((8, LANES), 1)
    reach = jnp.where(kind % 4 < 2, LANES - c, c + 1).astype(F32)
    basis = jnp.exp(-reach / col_scale) * jnp.where(kind % 2 == 0, 1.0, reach / LANES)
    high = basis.astype(BF16)
    basis = jnp.where(kind < 4, high.astype(F32), basis - high.astype(F32)).astype(BF16)
    m_lane = iota((1, LANES), 1)
    cell = jnp.full((1, LANES), -1, jnp.int32)
    batches, per_batch = cells_ref.shape
    for b in range(batches):
        for n in range(per_batch):
            cell = jnp.where(m_lane == b * per_batch + n, cells_ref[b, n], cell)
    cell_row, cell_col = lax.div(cell, total_cols), lax.rem(cell, total_cols)
    row_weight = factor(cell_row - iota((rows, LANES), 0), row_scale, row_reach)
    row_weight = row_weight.astype(BF16).astype(F32)
    col_weight = factor(
        cell_col - (col * LANES + iota((LANES, LANES), 0)), col_scale, col_reach
    ).astype(BF16)
    mom_ref[...] = jnp.zeros(mom_ref.shape, F32)
    for w in range(wells):
        for g in range(groups):
            tiles = []
            for t in range(0, seg, 8):
                at = (t + 1) * 16 + g * wells + w
                tiles.append(jnp.concatenate(
                    [x_ref[pl.ds(at + 8 * p, 8, stride=16), :] for p in range(2)], axis=1
                ))
            value = dot(jnp.concatenate(tiles, axis=0).astype(BF16), order)
            if g % 2 == 1:
                value = dot(reverse, value.astype(BF16))
            adj_ref[w, g * seg : (g + 1) * seg, :] = value.astype(BF16)
        adjoint = adj_ref[w]
        both = lax.dot_general(
            basis, adjoint, (((1,), (1,)), ((), ())), preferred_element_type=F32
        )
        mom_ref[0:4, w * rows : (w + 1) * rows] = both[0:4] + both[4:8]
        sampled = jnp.sum(dot(adjoint, col_weight) * row_weight, axis=0, keepdims=True)
        mom_ref[4:5, w * rows : w * rows + LANES] = sampled


def mix_kernel(offsets, swapped, tiles, place_ref, corr_ref, taper_ref, adj_ref, mom_ref, *refs):
    tile_refs = refs[:tiles]
    out_refs = refs[tiles:]
    wells, rows, _ = adj_ref.shape
    col, taper = place_ref[1], taper_ref[1]
    row_scale, row_reach, col_scale, col_reach = scales(corr_ref, taper_ref, rows)
    ones = jnp.ones((1, LANES), F32)
    scale_v, reach_v = ones * col_scale, ones * col_reach
    sums = [jnp.zeros((1, wells * rows), F32) for _ in range(4)]
    for index, offset in enumerate(offsets):
        if offset == 0:
            continue
        away = lax.bitwise_xor(col, offset) - col
        for side, k in ((0, -away), (1, away)):
            live = (k >= 1) & (k < taper)
            gap = jnp.maximum(k - 1, 0).astype(F32)
            gain = jnp.where(live, 1.0, 0.0) * jnp.exp(-gap * LANES / scale_v)
            gain = gain[:, :1]
            zero = mom_ref[index, 2 * side : 2 * side + 1, :]
            one = mom_ref[index, 2 * side + 1 : 2 * side + 2, :]
            sums[2 * side] = sums[2 * side] + gain * zero
            sums[2 * side + 1] = sums[2 * side + 1] + gain * (gap * zero + one)
    stacked = jnp.concatenate(sums * 4, axis=0)
    kind = iota((16, wells * rows), 0)
    high = stacked.astype(BF16).astype(F32)
    stacked = jnp.where((kind >= 4) & (kind < 8), stacked - high, high).astype(BF16)
    kind, c = iota((16, LANES), 0), iota((16, LANES), 1)
    near = jnp.where(kind % 4 < 2, c, LANES - 1 - c).astype(F32)
    spread = jnp.exp(-near / col_scale) * jnp.where(
        kind % 2 == 0, 1.0 - near / col_reach, -LANES / col_reach
    )
    high = spread.astype(BF16).astype(F32)
    spread = jnp.where(kind < 8, high, jnp.where(kind < 12, spread - high, 0.0)).astype(BF16)
    src, dst = iota((LANES, LANES), 0), iota((LANES, LANES), 1)
    matrices = [factor(dst - src, col_scale, col_reach).astype(BF16)]
    even = lax.rem(lax.div(col, taper), 2) == 0
    shift = jnp.where(even, taper, -taper) * LANES
    for i in range(tiles):
        matrices.append(
            factor(dst - src - (shift if i == 0 else -shift), col_scale, col_reach).astype(BF16)
        )
    row_mix = factor(
        iota((rows, rows), 0) - iota((rows, rows), 1), row_scale, row_reach
    ).astype(BF16)
    for w in range(wells):
        mixed = lax.dot_general(
            stacked[:, w * rows : (w + 1) * rows], spread,
            (((0,), (0,)), ((), ())), preferred_element_type=F32,
        )
        mixed = mixed + dot(adj_ref[w], matrices[0])
        for ref, matrix in zip(tile_refs, matrices[1:]):
            mixed = mixed + dot(ref[w], matrix)
        field = dot(row_mix, mixed.astype(BF16)).astype(BF16)
        if swapped:
            half = rows // 2
            keep = place_ref[0] == 0
            out_refs[0][w] = jnp.where(keep, field[:half], field[half:])
            out_refs[1][w] = jnp.where(keep, field[half:], field[:half])
        else:
            out_refs[0][w] = field


VMEM = pl.BlockSpec(memory_space=pltpu.VMEM)
SMEM = pl.BlockSpec(memory_space=pltpu.SMEM)


def call(kernel, smem, vmem, outs, scratch=(), flops=1):
    return pl.pallas_call(
        kernel,
        in_specs=[SMEM] * len(smem) + [VMEM] * len(vmem),
        out_specs=[VMEM] * len(outs),
        out_shape=[jax.ShapeDtypeStruct(shape, dtype) for shape, dtype in outs],
        scratch_shapes=list(scratch),
        compiler_params=pltpu.CompilerParams(vmem_limit_bytes=48 * 2**20),
        cost_estimate=pl.CostEstimate(flops=flops, bytes_accessed=2**20, transcendentals=0),
    )(*smem, *vmem)


def pairs_at(count, distance, odd):
    pairs = []
    for i in range(count - distance):
        if (i // distance) % 2 == odd:
            pairs += [(i, i + distance), (i + distance, i)]
    return pairs


def exchanged(value, axis):
    return lax.ppermute(value, axis, [(0, 1), (1, 0)])


def local(log_trans, corr_len, taper_width, well_cells, obs_weight):
    tile_rows, tile_cols = log_trans.shape
    row_count, col_count = lax.axis_size("row"), lax.axis_size("col")
    total_rows, total_cols = tile_rows * row_count, tile_cols * col_count
    well_count = well_cells.shape[1]
    wells = well_count // row_count
    row, col = lax.axis_index("row"), lax.axis_index("col")
    place = jnp.stack([row, col]).astype(jnp.int32)
    own = obs_weight[0]
    swapped = row_count == 2
    tile = (wells, total_rows, tile_cols)

    if swapped:
        other_logs = exchanged(log_trans, "row")
        sent = lax.dynamic_slice_in_dim(own, (1 - row) * wells, wells, axis=0)
        operands = (own, exchanged(sent, "row"), log_trans, other_logs)
    else:
        operands = (
            lax.all_to_all(own, "row", 0, 1, tiled=True),
            lax.all_gather(log_trans, "row", axis=0, tiled=True),
        )
    strip = ((total_rows, 2 * LANES), BF16)
    full, split, strip_a, strip_b = call(
        functools.partial(pack_kernel, swapped), (place,), operands,
        [(tile, BF16), ((3,) + tile[1:], BF16), strip, strip],
    )
    strip_a = lax.ppermute(strip_a, "col", pairs_at(col_count, 1, 0))
    strip_b = lax.ppermute(strip_b, "col", pairs_at(col_count, 1, 1))

    seg = total_rows * wells // 8
    adjoint, moments = call(
        functools.partial(sweep_kernel, total_cols),
        (place, corr_len, taper_width, well_cells), (full, split, strip_a, strip_b),
        [(tile, BF16), ((8, wells * total_rows), F32)],
        [
            pltpu.VMEM((total_rows + 16, 2 * LANES), F32),
            pltpu.VMEM(((seg + 2) * 16, LANES), F32),
            pltpu.VMEM((seg * 16, LANES), F32),
            pltpu.VMEM((seg * 64, LANES), F32),
        ],
    )

    def finish(distance, adjoint, moments):
        tiles = []
        for odd in range(2):
            pairs = pairs_at(col_count, distance, odd)
            if pairs:
                tiles.append(lax.ppermute(adjoint, "col", pairs))
        gathered, offsets = moments[None], [0]
        step = col_count // 2
        while step:
            moved = lax.ppermute(gathered, "col", [(i, i ^ step) for i in range(col_count)])
            gathered = jnp.concatenate([gathered, moved], axis=0)
            offsets = offsets + [offset ^ step for offset in offsets]
            step //= 2
        samples = [gathered[i, 4] for i in range(col_count)]
        while len(samples) > 1:
            samples = [a + b for a, b in zip(samples[::2], samples[1::2])]
        samples = samples[0].reshape(wells, total_rows)[:, : 2 * well_count]
        samples = lax.all_gather(samples, "row", axis=0, tiled=True)
        samples = lax.all_gather(samples, "sect", axis=0, tiled=True)
        half = ((wells, tile_rows, tile_cols), BF16)
        fields = call(
            functools.partial(mix_kernel, tuple(offsets), swapped, len(tiles)),
            (place, corr_len, taper_width), (adjoint, gathered, *tiles),
            [half, half] if swapped else [(tile, BF16)],
        )
        return tuple(fields) + (samples.T,)

    branches = [functools.partial(finish, distance) for distance in range(1, TAPER + 1)]
    *fields, measure_cov = lax.switch(taper_width[1] - 1, branches, adjoint, moments)
    if swapped:
        kept, sent = fields
        other = exchanged(sent, "row")
        low = row == 0
        qh_fields = jnp.concatenate(
            [jnp.where(low, kept, other), jnp.where(low, other, kept)], axis=0
        )
    else:
        qh_fields = lax.all_to_all(fields[0], "row", 1, 0, tiled=True)
    return (qh_fields[None], measure_cov)


def solution(mesh):
    placed = (P("row", "col"), P(), P(), P(), P("sect", None, "row", "col"))
    return jax.shard_map(
        local,
        mesh=mesh,
        in_specs=placed,
        out_specs=(P("sect", None, "row", "col"), P()),
        check_vma=False,
    )
```

```python
import functools

import jax
import jax.numpy as jnp
from jax import lax
from jax.experimental import pallas as pl
from jax.experimental.pallas import tpu as pltpu
from jax.sharding import PartitionSpec as P

BLOCK = 128
TAPER = 4
SWEEPS = 24
HALO = 24
LANES = 128
STRIP = 32
UNROLL = 64

leakage = 0.05
F32, BF16 = jnp.float32, jnp.bfloat16


def iota(shape, dim):
    return lax.broadcasted_iota(jnp.int32, shape, dim)


def one_hot(mask):
    return jnp.where(mask, 1.0, 0.0).astype(BF16)


def dot(a, b):
    return jnp.dot(a, b, preferred_element_type=F32)


def harmonic(a, b):
    return 2.0 * a * b / (a + b)


def factor(offset, scale, reach):
    distance = jnp.abs(offset).astype(F32)
    return jnp.exp(-distance / scale) * jnp.maximum(1.0 - distance / reach, 0.0)


def scales(corr_ref, taper_ref, total_rows):
    row_scale = corr_ref[0] * (total_rows / 4.0)
    row_reach = (taper_ref[0] + TAPER).astype(F32) * (total_rows / (2.0 * TAPER)) + 1.0
    col_scale = corr_ref[1] * BLOCK
    col_reach = (taper_ref[1] * BLOCK + 1).astype(F32)
    return row_scale, row_reach, col_scale, col_reach


def pack_kernel(swapped, place_ref, *refs):
    if swapped:
        obs_ref, recv_ref, lt_ref, lt_recv_ref, full_ref, split_ref, a_ref, b_ref = refs
    else:
        obs_ref, lt_ref, full_ref, split_ref, a_ref, b_ref = refs
    wells, rows, _ = full_ref.shape
    if swapped:
        half = rows // 2
        mine = pl.multiple_of(place_ref[0] * half, half)
        other = pl.multiple_of(half - mine, half)
        first = place_ref[0] * wells
        for w in range(wells):
            full_ref[w, pl.ds(mine, half), :] = obs_ref[first + w]
            full_ref[w, pl.ds(other, half), :] = recv_ref[w]
        parts = [(lt_ref[...], pl.ds(mine, half)), (lt_recv_ref[...], pl.ds(other, half))]
    else:
        full_ref[...] = obs_ref[...]
        parts = [(lt_ref[...], pl.ds(0, rows))]
    for value, where in parts:
        for i in range(3):
            piece = value.astype(BF16)
            split_ref[i, where, :] = piece
            value = value - piece.astype(F32)
    even = lax.rem(place_ref[1], 2) == 0
    src, dst = iota((LANES, LANES), 0), iota((LANES, LANES), 1)
    tail = LANES - HALO
    start_a = jnp.where(even, tail, 0)
    for out_ref, start in ((a_ref, start_a), (b_ref, tail - start_a)):
        for group, (ref, count) in enumerate(((full_ref, wells), (split_ref, 3))):
            total = jnp.zeros((rows, LANES), F32)
            for i in range(count):
                k = dst - STRIP * i
                pick = one_hot((src == k + start) & (k >= 0) & (k < HALO))
                total = total + dot(ref[i], pick)
            out_ref[:, group * LANES : (group + 1) * LANES] = total.astype(BF16)


def pair_swap(value, wells, outer):
    groups = 8 // wells
    group = iota(value.shape, 0) // wells
    up = pltpu.roll(value, wells, 0)
    if groups == 2:
        return up
    down = pltpu.roll(value, 8 - wells, 0)
    return jnp.where((group % 2 == 0) == (not outer), down, up)


def update(previous, current, following, coefs, source):
    result = []
    even, odd = current
    sides = ((odd, pltpu.roll(odd, 1, 1)), (pltpu.roll(even, LANES - 1, 1), even))
    for p in range(2):
        ce, cw, co, ci = coefs[4 * p : 4 * p + 4]
        east, west = sides[p]
        result.append(
            (source[p] + ce * east) + (cw * west + co * previous[p]) + ci * following[p]
        )
    return result


def sweep_kernel(total_cols, place_ref, corr_ref, taper_ref, cells_ref,
                 full_ref, split_ref, a_ref, b_ref, adj_ref, mom_ref,
                 nat_ref, xa_ref, xb_ref, s_ref, c_ref):
    wells, rows, _ = full_ref.shape
    groups = 8 // wells
    seg = rows // groups
    col = place_ref[1]
    even = lax.rem(col, 2) == 0
    src, dst = iota((LANES, 2 * LANES), 0), iota((LANES, 2 * LANES), 1)
    window = 2 * (dst % LANES) + dst // LANES
    own_pick = one_hot(window == src + HALO)
    right = LANES + HALO
    base_a = jnp.where(even, right, 0)
    picks = []
    for i in range(max(wells, 3)):
        k = src - STRIP * i
        live = (k >= 0) & (k < HALO)
        picks.append(tuple(
            one_hot((window == k + base) & live) for base in (base_a, right - base_a)
        ))

    def widened(ref, i, group):
        lanes = slice(group * LANES, (group + 1) * LANES)
        return (
            dot(ref[i], own_pick)
            + dot(a_ref[:, lanes], picks[i][0])
            + dot(b_ref[:, lanes], picks[i][1])
        )

    planes = [widened(split_ref, i, 1) for i in range(3)]
    nat_ref[0:8, :] = jnp.zeros((8, 2 * LANES), F32)
    nat_ref[rows + 8 : rows + 16, :] = jnp.zeros((8, 2 * LANES), F32)
    nat_ref[8 : rows + 8, :] = planes[0] + planes[1] + planes[2]
    planes = [plane.astype(BF16) for plane in planes]
    fields = [widened(full_ref, w, 0) for w in range(wells)]

    lane = iota((seg, LANES), 1)
    step = iota((seg, LANES), 0)
    t_pick, r_pick = iota((seg + 16, rows), 0), iota((seg + 16, rows), 1)
    t_flip, r_flip = iota((seg, rows), 0), iota((seg, rows), 1)
    for g in range(groups):
        if g % 2 == 0:
            logs = nat_ref[g * seg : g * seg + seg + 16, :]
        else:
            pick = one_hot(r_pick == (g + 1) * seg - 1 - (t_pick - 8))
            logs = dot(pick, planes[0]) + dot(pick, planes[1]) + dot(pick, planes[2])
            flip = one_hot(r_flip == (g + 1) * seg - 1 - t_flip)
        cond = jnp.exp(logs)
        sides = [cond[:, :LANES], cond[:, LANES:]]
        centre = [side[8 : seg + 8] for side in sides]
        east = (centre[1], pltpu.roll(centre[0], LANES - 1, 1))
        west = (pltpu.roll(centre[1], 1, 1), centre[0])
        edge = (step == 0) if g in (0, groups - 1) else None
        inverse = []
        for p in range(2):
            column = col * LANES - HALO + 2 * lane + p
            inside = (column >= 0) & (column < total_cols) & (lane < (LANES + 2 * HALO) // 2)
            has_east, has_west = column < total_cols - 1, column > 0
            mid = centre[p]
            fe = jnp.where(has_east, harmonic(mid, east[p]), mid)
            fw = jnp.where(has_west, harmonic(mid, west[p]), mid)
            fo = harmonic(mid, sides[p][7 : seg + 7])
            if edge is not None:
                fo = jnp.where(edge, mid, fo)
            fi = harmonic(mid, sides[p][9 : seg + 9])
            inv = jnp.where(inside, 1.0 / (fe + fw + fo + fi + leakage), 0.0)
            inverse.append(inv)
            outer = fo * inv
            if edge is not None:
                outer = jnp.where(edge, 0.0, outer)
            coefs = (
                jnp.where(has_east, fe * inv, 0.0),
                jnp.where(has_west, fw * inv, 0.0),
                outer,
                fi * inv,
            )
            for d, coef in enumerate(coefs):
                for t in range(0, seg, 8):
                    for w in range(wells):
                        at = ((t * 2 + p) * 4 + d) * 8 + g * wells + w
                        c_ref[pl.ds(at, 8, stride=64), :] = coef[t : t + 8]
        for w in range(wells):
            if g % 2 == 0:
                field = fields[w][g * seg : (g + 1) * seg]
            else:
                field = dot(flip, fields[w].astype(BF16))
            for p in range(2):
                value = field[:, p * LANES : (p + 1) * LANES] * inverse[p]
                for t in range(0, seg, 8):
                    at = (t * 2 + p) * 8 + g * wells + w
                    s_ref[pl.ds(at, 8, stride=16), :] = value[t : t + 8]

    def load(ref, t, count=2):
        at = pl.multiple_of(t * (count * 8), count * 8)
        return [ref[pl.ds(at + 8 * i, 8), :] for i in range(count)]

    def save(ref, t, value):
        at = pl.multiple_of(t * 16, 16)
        for p in range(2):
            ref[pl.ds(at + 8 * p, 8), :] = value[p]

    def march(from_ref, to_ref):
        x1 = load(from_ref, 0)
        x0 = [pair_swap(v, wells, True) for v in x1]
        save(from_ref, seg, [pair_swap(v, wells, False) for v in load(from_ref, seg - 1)])

        def rows_of(block, carry):
            x0, x1 = carry
            for i in range(UNROLL):
                t = block * UNROLL + i
                x2 = load(from_ref, t + 1)
                save(to_ref, t, update(x0, x1, x2, load(c_ref, t, 8), load(s_ref, t)))
                x0, x1 = x1, x2
            return x0, x1

        lax.fori_loop(0, seg // UNROLL, rows_of, (x0, x1))

    march(s_ref, xa_ref)

    def more(_, carry):
        march(xa_ref, xb_ref)
        march(xb_ref, xa_ref)
        return carry

    lax.fori_loop(0, SWEEPS // 2 - 1, more, 0)

    row_scale, row_reach, col_scale, col_reach = scales(corr_ref, taper_ref, rows)
    order = one_hot(
        2 * (iota((2 * LANES, LANES), 0) % LANES) + iota((2 * LANES, LANES), 0) // LANES
        == iota((2 * LANES, LANES), 1) + HALO
    )
    reverse = one_hot(iota((seg, seg), 0) == seg - 1 - iota((seg, seg), 1))
    kind, c = iota((8, LANES), 0), iota((8, LANES), 1)
    reach = jnp.where(kind % 4 < 2, LANES - c, c + 1).astype(F32)
    basis = jnp.exp(-reach / col_scale) * jnp.where(kind % 2 == 0, 1.0, reach / LANES)
    high = basis.astype(BF16)
    basis = jnp.where(kind < 4, high.astype(F32), basis - high.astype(F32)).astype(BF16)
    m_lane = iota((1, LANES), 1)
    cell = jnp.full((1, LANES), -1, jnp.int32)
    batches, per_batch = cells_ref.shape
    for b in range(batches):
        for n in range(per_batch):
            cell = jnp.where(m_lane == b * per_batch + n, cells_ref[b, n], cell)
    cell_row, cell_col = lax.div(cell, total_cols), lax.rem(cell, total_cols)
    row_weight = factor(cell_row - iota((rows, LANES), 0), row_scale, row_reach)
    row_weight = row_weight.astype(BF16).astype(F32)
    col_weight = factor(
        cell_col - (col * LANES + iota((LANES, LANES), 0)), col_scale, col_reach
    ).astype(BF16)
    mom_ref[...] = jnp.zeros(mom_ref.shape, F32)
    for w in range(wells):
        for g in range(groups):
            tiles = []
            for t in range(0, seg, 8):
                at = t * 16 + g * wells + w
                tiles.append(jnp.concatenate(
                    [xa_ref[pl.ds(at + 8 * p, 8, stride=16), :] for p in range(2)], axis=1
                ))
            value = dot(jnp.concatenate(tiles, axis=0).astype(BF16), order)
            if g % 2 == 1:
                value = dot(reverse, value.astype(BF16))
            adj_ref[w, g * seg : (g + 1) * seg, :] = value.astype(BF16)
        adjoint = adj_ref[w]
        both = lax.dot_general(
            basis, adjoint, (((1,), (1,)), ((), ())), preferred_element_type=F32
        )
        mom_ref[0:4, w * rows : (w + 1) * rows] = both[0:4] + both[4:8]
        sampled = jnp.sum(dot(adjoint, col_weight) * row_weight, axis=0, keepdims=True)
        mom_ref[4:5, w * rows : w * rows + LANES] = sampled


def mix_kernel(offsets, swapped, tiles, place_ref, corr_ref, taper_ref, adj_ref, mom_ref, *refs):
    tile_refs = refs[:tiles]
    out_refs = refs[tiles:]
    wells, rows, _ = adj_ref.shape
    col, taper = place_ref[1], taper_ref[1]
    row_scale, row_reach, col_scale, col_reach = scales(corr_ref, taper_ref, rows)
    ones = jnp.ones((1, LANES), F32)
    scale_v, reach_v = ones * col_scale, ones * col_reach
    sums = [jnp.zeros((1, wells * rows), F32) for _ in range(4)]
    for index, offset in enumerate(offsets):
        if offset == 0:
            continue
        away = lax.bitwise_xor(col, offset) - col
        for side, k in ((0, -away), (1, away)):
            live = (k >= 1) & (k < taper)
            gap = jnp.maximum(k - 1, 0).astype(F32)
            gain = jnp.where(live, 1.0, 0.0) * jnp.exp(-gap * LANES / scale_v)
            gain = gain[:, :1]
            zero = mom_ref[index, 2 * side : 2 * side + 1, :]
            one = mom_ref[index, 2 * side + 1 : 2 * side + 2, :]
            sums[2 * side] = sums[2 * side] + gain * zero
            sums[2 * side + 1] = sums[2 * side + 1] + gain * (gap * zero + one)
    stacked = jnp.concatenate(sums * 4, axis=0)
    kind = iota((16, wells * rows), 0)
    high = stacked.astype(BF16).astype(F32)
    stacked = jnp.where((kind >= 4) & (kind < 8), stacked - high, high).astype(BF16)
    kind, c = iota((16, LANES), 0), iota((16, LANES), 1)
    near = jnp.where(kind % 4 < 2, c, LANES - 1 - c).astype(F32)
    spread = jnp.exp(-near / col_scale) * jnp.where(
        kind % 2 == 0, 1.0 - near / col_reach, -LANES / col_reach
    )
    high = spread.astype(BF16).astype(F32)
    spread = jnp.where(kind < 8, high, jnp.where(kind < 12, spread - high, 0.0)).astype(BF16)
    src, dst = iota((LANES, LANES), 0), iota((LANES, LANES), 1)
    matrices = [factor(dst - src, col_scale, col_reach).astype(BF16)]
    even = lax.rem(lax.div(col, taper), 2) == 0
    shift = jnp.where(even, taper, -taper) * LANES
    for i in range(tiles):
        matrices.append(
            factor(dst - src - (shift if i == 0 else -shift), col_scale, col_reach).astype(BF16)
        )
    row_mix = factor(
        iota((rows, rows), 0) - iota((rows, rows), 1), row_scale, row_reach
    ).astype(BF16)
    for w in range(wells):
        mixed = lax.dot_general(
            stacked[:, w * rows : (w + 1) * rows], spread,
            (((0,), (0,)), ((), ())), preferred_element_type=F32,
        )
        mixed = mixed + dot(adj_ref[w], matrices[0])
        for ref, matrix in zip(tile_refs, matrices[1:]):
            mixed = mixed + dot(ref[w], matrix)
        field = dot(row_mix, mixed.astype(BF16)).astype(BF16)
        if swapped:
            half = rows // 2
            keep = place_ref[0] == 0
            out_refs[0][w] = jnp.where(keep, field[:half], field[half:])
            out_refs[1][w] = jnp.where(keep, field[half:], field[:half])
        else:
            out_refs[0][w] = field


VMEM = pl.BlockSpec(memory_space=pltpu.VMEM)
SMEM = pl.BlockSpec(memory_space=pltpu.SMEM)


def call(kernel, smem, vmem, outs, scratch=(), flops=1):
    return pl.pallas_call(
        kernel,
        in_specs=[SMEM] * len(smem) + [VMEM] * len(vmem),
        out_specs=[VMEM] * len(outs),
        out_shape=[jax.ShapeDtypeStruct(shape, dtype) for shape, dtype in outs],
        scratch_shapes=list(scratch),
        compiler_params=pltpu.CompilerParams(vmem_limit_bytes=48 * 2**20),
        cost_estimate=pl.CostEstimate(flops=flops, bytes_accessed=2**20, transcendentals=0),
    )(*smem, *vmem)


def pairs_at(count, distance, odd):
    pairs = []
    for i in range(count - distance):
        if (i // distance) % 2 == odd:
            pairs += [(i, i + distance), (i + distance, i)]
    return pairs


def exchanged(value, axis):
    return lax.ppermute(value, axis, [(0, 1), (1, 0)])


def local(log_trans, corr_len, taper_width, well_cells, obs_weight):
    tile_rows, tile_cols = log_trans.shape
    row_count, col_count = lax.axis_size("row"), lax.axis_size("col")
    total_rows, total_cols = tile_rows * row_count, tile_cols * col_count
    well_count = well_cells.shape[1]
    wells = well_count // row_count
    row, col = lax.axis_index("row"), lax.axis_index("col")
    place = jnp.stack([row, col]).astype(jnp.int32)
    own = obs_weight[0]
    swapped = row_count == 2
    tile = (wells, total_rows, tile_cols)

    if swapped:
        other_logs = exchanged(log_trans, "row")
        sent = lax.dynamic_slice_in_dim(own, (1 - row) * wells, wells, axis=0)
        operands = (own, exchanged(sent, "row"), log_trans, other_logs)
    else:
        operands = (
            lax.all_to_all(own, "row", 0, 1, tiled=True),
            lax.all_gather(log_trans, "row", axis=0, tiled=True),
        )
    strip = ((total_rows, 2 * LANES), BF16)
    full, split, strip_a, strip_b = call(
        functools.partial(pack_kernel, swapped), (place,), operands,
        [(tile, BF16), ((3,) + tile[1:], BF16), strip, strip],
    )
    strip_a = lax.ppermute(strip_a, "col", pairs_at(col_count, 1, 0))
    strip_b = lax.ppermute(strip_b, "col", pairs_at(col_count, 1, 1))

    seg = total_rows * wells // 8
    adjoint, moments = call(
        functools.partial(sweep_kernel, total_cols),
        (place, corr_len, taper_width, well_cells), (full, split, strip_a, strip_b),
        [(tile, BF16), ((8, wells * total_rows), F32)],
        [
            pltpu.VMEM((total_rows + 16, 2 * LANES), F32),
            pltpu.VMEM(((seg + 2) * 16, LANES), F32),
            pltpu.VMEM(((seg + 2) * 16, LANES), F32),
            pltpu.VMEM(((seg + 2) * 16, LANES), F32),
            pltpu.VMEM((seg * 64, LANES), F32),
        ],
    )

    def finish(distance, adjoint, moments):
        tiles = []
        for odd in range(2):
            pairs = pairs_at(col_count, distance, odd)
            if pairs:
                tiles.append(lax.ppermute(adjoint, "col", pairs))
        gathered, offsets = moments[None], [0]
        step = col_count // 2
        while step:
            moved = lax.ppermute(gathered, "col", [(i, i ^ step) for i in range(col_count)])
            gathered = jnp.concatenate([gathered, moved], axis=0)
            offsets = offsets + [offset ^ step for offset in offsets]
            step //= 2
        half = ((wells, tile_rows, tile_cols), BF16)
        fields = call(
            functools.partial(mix_kernel, tuple(offsets), swapped, len(tiles)),
            (place, corr_len, taper_width), (adjoint, gathered, *tiles),
            [half, half] if swapped else [(tile, BF16)],
        )
        samples, *fields = lax.optimization_barrier((gathered[:, 4], *fields))
        if swapped:
            kept, sent = fields
            other = exchanged(sent, "row")
        samples = [samples[i] for i in range(col_count)]
        while len(samples) > 1:
            samples = [a + b for a, b in zip(samples[::2], samples[1::2])]
        samples = samples[0].reshape(wells, total_rows)[:, : 2 * well_count]
        if swapped:
            theirs = exchanged(samples, "row")
            low = row == 0
            samples = jnp.concatenate(
                [jnp.where(low, samples, theirs), jnp.where(low, theirs, samples)], axis=0
            )
            qh_fields = jnp.concatenate(
                [jnp.where(low, kept, other), jnp.where(low, other, kept)], axis=0
            )
        else:
            samples = lax.all_gather(samples, "row", axis=0, tiled=True)
            qh_fields = lax.all_to_all(fields[0], "row", 1, 0, tiled=True)
        samples = lax.all_gather(samples, "sect", axis=0, tiled=True)
        return qh_fields[None], samples.T

    branches = [functools.partial(finish, distance) for distance in range(1, TAPER + 1)]
    return lax.switch(taper_width[1] - 1, branches, adjoint, moments)


def solution(mesh):
    placed = (P("row", "col"), P(), P(), P(), P("sect", None, "row", "col"))
    return jax.shard_map(
        local,
        mesh=mesh,
        in_specs=placed,
        out_specs=(P("sect", None, "row", "col"), P()),
        check_vma=False,
    )
```

```python
import functools

import jax
import jax.numpy as jnp
from jax import lax
from jax.experimental import pallas as pl
from jax.experimental.pallas import tpu as pltpu
from jax.sharding import PartitionSpec as P

BLOCK = 128
TAPER = 4
SWEEPS = 24
HALO = 24
LANES = 128
STRIP = 32
PACK = LANES // STRIP
CHUNKS = 1
UNROLL = 16

leakage = 0.05
F32, BF16 = jnp.float32, jnp.bfloat16


def iota(shape, dim):
    return lax.broadcasted_iota(jnp.int32, shape, dim)


def one_hot(mask):
    return jnp.where(mask, 1.0, 0.0).astype(BF16)


def dot(a, b):
    return jnp.dot(a, b, preferred_element_type=F32)


def harmonic(a, b):
    return 2.0 * a * b / (a + b)


def factor(offset, scale, reach):
    distance = jnp.abs(offset).astype(F32)
    return jnp.exp(-distance / scale) * jnp.maximum(1.0 - distance / reach, 0.0)


def scales(corr_ref, taper_ref, total_rows):
    row_scale = corr_ref[0] * (total_rows / 4.0)
    row_reach = (taper_ref[0] + TAPER).astype(F32) * (total_rows / (2.0 * TAPER)) + 1.0
    col_scale = corr_ref[1] * BLOCK
    col_reach = (taper_ref[1] * BLOCK + 1).astype(F32)
    return row_scale, row_reach, col_scale, col_reach


def split3(value):
    pieces = []
    for _ in range(3):
        piece = value.astype(BF16)
        pieces.append(piece)
        value = value - piece.astype(F32)
    return pieces


def strip_slot(lane, wells):
    slot, k = lane // HALO, lane % HALO
    return jnp.where(slot <= wells, slot, -1), k


def strips(place_ref, fields, logs):
    even = lax.rem(place_ref[1], 2) == 0
    tail = LANES - HALO
    start_a = jnp.where(even, tail, 0)
    rows = fields[0].shape[0]
    values = jnp.concatenate(fields + [logs[0]], axis=1)
    shape = (values.shape[1], 2 * LANES)
    src, dst = iota(shape, 0), iota(shape, 1)
    slot, k = strip_slot(dst % LANES, len(fields))
    start = jnp.where(dst < LANES, start_a, tail - start_a)
    first = dot(values, one_hot((slot == src // LANES) & (src % LANES == k + start)))
    shape = (LANES, 2 * LANES)
    src, dst = iota(shape, 0), iota(shape, 1)
    start = jnp.where(dst < LANES, start_a, tail - start_a)
    k = dst % STRIP
    wide = dot(logs[1], one_hot((src == k + start) & (k < HALO)))
    block = rows // PACK
    lane = iota((block, 2 * LANES), 1) % LANES // STRIP
    second = jnp.zeros((block, 2 * LANES), F32)
    for q in range(PACK):
        second = jnp.where(lane == q, wide[q * block : (q + 1) * block], second)
    return [
        (first[:, at : at + LANES].astype(BF16), second[:, at : at + LANES].astype(BF16))
        for at in (0, LANES)
    ]


def split_kernel(place_ref, obs_ref, lt_ref, sent_ref, kept_ref, planes_ref, logs_ref, sems):
    wells = sent_ref.shape[0]
    mine = place_ref[0] * wells
    copies = [
        pltpu.make_async_copy(lt_ref, logs_ref, sems.at[0]),
        pltpu.make_async_copy(obs_ref.at[pl.ds(wells - mine, wells)], sent_ref, sems.at[1]),
        pltpu.make_async_copy(obs_ref.at[pl.ds(mine, wells)], kept_ref, sems.at[2]),
    ]
    for copy in copies:
        copy.start()
    copies[0].wait()
    for i, piece in enumerate(split3(logs_ref[...])):
        planes_ref[i] = piece
    copies[1].wait()
    copies[2].wait()


def row_parts(swapped, place_ref, refs, rows):
    if not swapped:
        obs_ref, lt_ref = refs
        return [(pl.ds(0, rows), [obs_ref[w] for w in range(obs_ref.shape[0])], split3(lt_ref[...]))]
    kept_ref, planes_ref, recv_ref, lt_ref = refs
    half = rows // 2
    mine = pl.multiple_of(place_ref[0] * half, half)
    other = pl.multiple_of(half - mine, half)
    wells = kept_ref.shape[0]
    return [
        (pl.ds(mine, half), [kept_ref[w] for w in range(wells)], [planes_ref[i] for i in range(3)]),
        (pl.ds(other, half), [recv_ref[w] for w in range(wells)], split3(lt_ref[...])),
    ]


def pack_kernel(swapped, place_ref, *refs):
    out_refs = refs[-2:]
    rows = out_refs[0].shape[0] * PACK // (PACK + 1)
    for where, fields, logs in row_parts(swapped, place_ref, refs[:-2], rows):
        block = where.size // PACK
        after = pl.multiple_of(rows + lax.div(where.start, PACK), 8)
        for ref, (first, second) in zip(out_refs, strips(place_ref, fields, logs)):
            ref[where, :] = first
            ref[pl.ds(after, block), :] = second


def layout(wells):
    width = LANES // wells
    return width, -(-(LANES + 2 * HALO) // width)


def fold_rows(rows, transposed=False):
    at, row = iota((rows, rows), int(transposed)), iota((rows, rows), 1 - int(transposed))
    seg = rows // 8
    t, g = at // 8, at % 8
    return one_hot(row == jnp.where(g % 2 == 0, g * seg + t, (g + 1) * seg - 1 - t))


def window_column(wells, shape, dim):
    width, parts = layout(wells)
    lane = iota(shape, dim)
    return parts * (lane % width) + lane // LANES, (lane % LANES) // width


def own_kernel(swapped, wells, total_cols, place_ref, corr_ref, taper_ref, cells_ref, *refs):
    field_ref, log_ref, basis_ref, rw_ref, cw_ref, all_ref = refs[-6:]
    rows = field_ref.shape[0]
    parts = layout(wells)[1]
    for where, fields, logs in row_parts(swapped, place_ref, refs[:-6], rows):
        for i, value in enumerate(fields + logs):
            all_ref[where, i * LANES : (i + 1) * LANES] = value
    folded = dot(fold_rows(rows), all_ref[...]).astype(BF16)
    edge = wells * LANES
    shape = (edge, parts * LANES)
    column, well = window_column(wells, shape, 1)
    src = iota(shape, 0)
    pick = one_hot((column == src % LANES + HALO) & (well == src // LANES))
    field_ref[...] = dot(folded[:, :edge], pick)
    shape = (3 * LANES, parts * LANES)
    column, _ = window_column(wells, shape, 1)
    pick = one_hot(column == iota(shape, 0) % LANES + HALO)
    log_ref[...] = dot(folded[:, edge:], pick)
    col = place_ref[1]
    row_scale, row_reach, col_scale, col_reach = scales(corr_ref, taper_ref, rows)
    kind, c = iota((8, LANES), 0), iota((8, LANES), 1)
    reach = jnp.where(kind % 4 < 2, LANES - c, c + 1).astype(F32)
    basis = jnp.exp(-reach / col_scale) * jnp.where(kind % 2 == 0, 1.0, reach / LANES)
    high = basis.astype(BF16)
    basis_ref[...] = jnp.where(kind < 4, high.astype(F32), basis - high.astype(F32)).astype(BF16)
    m_lane = iota((1, LANES), 1)
    cell = jnp.full((1, LANES), -1, jnp.int32)
    batches, per_batch = cells_ref.shape
    for b in range(batches):
        for n in range(per_batch):
            cell = jnp.where(m_lane == b * per_batch + n, cells_ref[b, n], cell)
    cell_row, cell_col = lax.div(cell, total_cols), lax.rem(cell, total_cols)
    row_weight = factor(cell_row - iota((rows, LANES), 0), row_scale, row_reach)
    rw_ref[...] = row_weight.astype(BF16).astype(F32)
    cw_ref[...] = factor(
        cell_col - (col * LANES + iota((LANES, LANES), 0)), col_scale, col_reach
    ).astype(BF16)


def seam(value, outer):
    group = iota(value.shape, 0)
    up = pltpu.roll(value, 1, 0)
    down = pltpu.roll(value, 7, 0)
    return jnp.where((group % 2 == 0) == (not outer), down, up)


def sweep_kernel(wells, tile_rows, total_cols, place_ref, field_ref, log_ref, basis_ref, rw_ref,
                 cw_ref, a_ref, b_ref, *refs):
    adj_refs = refs[:-5]
    mom_ref, xa_ref, xb_ref, s_ref, c_ref = refs[-5:]
    rows = field_ref.shape[0]
    seg = rows // 8
    width, parts = layout(wells)
    col = place_ref[1]
    even = lax.rem(col, 2) == 0
    a, b = a_ref[...], b_ref[...]
    sides = []
    for side in (jnp.where(even, b, a), jnp.where(even, a, b)):
        block = tile_rows // PACK
        blank = jnp.zeros((block, LANES), BF16)
        quarter = iota((block, LANES), 1) // STRIP
        second = [
            jnp.where(quarter == q, side[rows + p * block : rows + (p + 1) * block], blank)
            for p in range(rows // tile_rows) for q in range(PACK)
        ]
        sides.append((side[:rows], jnp.concatenate(second, axis=0)))
    strip = jnp.concatenate([sides[0][0], sides[1][0], sides[0][1], sides[1][1]], axis=1)
    folded = dot(fold_rows(rows), strip).astype(BF16)
    shape = (2 * LANES, parts * LANES)
    column, well = window_column(wells, shape, 1)
    src = iota(shape, 0)
    base = jnp.where(src < LANES, 0, LANES + HALO)
    slot, k = strip_slot(src % LANES, wells)
    hit = column == k + base
    k = src % STRIP
    again = (k < HALO) & (column == k + base)
    fields = field_ref[...] + dot(folded[:, : 2 * LANES], one_hot(hit & (slot == well)))
    logs = log_ref[...] + dot(folded[:, : 2 * LANES], one_hot(hit & (slot == wells)))
    logs = logs + dot(folded[:, 2 * LANES :], one_hot(again))

    cond = jnp.exp(logs)
    cond = [cond[:, i * LANES : (i + 1) * LANES] for i in range(parts)]
    lane = iota((1, LANES), 1)
    group = iota((8, LANES), 0)
    border = (group == 0) | (group == 7)
    east = [harmonic(cond[i], cond[i + 1]) for i in range(parts - 1)]
    east.append(harmonic(cond[-1], pltpu.roll(cond[0], LANES - 1, 1)))
    west = [pltpu.roll(east[-1], 1, 1)] + east[:-1]
    for i in range(parts):
        place = parts * (lane % width) + i
        column = col * LANES - HALO + place
        inside = (column >= 0) & (column < total_cols) & (place < LANES + 2 * HALO)
        here = cond[i]
        inner = harmonic(here, jnp.concatenate([here[8:], seam(here[-8:], False)], axis=0))
        first = harmonic(here[:8], seam(here[:8], True))
        outer = jnp.concatenate([jnp.where(border, here[:8], first), inner[:-8]], axis=0)
        fe = jnp.where(column < total_cols - 1, east[i], here)
        fw = jnp.where(column > 0, west[i], here)
        inverse = jnp.where(inside, 1.0 / (fe + fw + outer + inner + leakage), 0.0)
        values = [fe * inverse, fw * inverse, outer * inverse, inner * inverse]
        source = fields[:, i * LANES : (i + 1) * LANES] * inverse
        for t in range(seg):
            s_ref[(t * parts + i) * 8 : (t * parts + i + 1) * 8, :] = source[8 * t : 8 * t + 8]
            for d in range(4):
                at = ((t * parts + i) * 4 + d) * 8
                value = values[d][8 * t : 8 * t + 8]
                if t == 0 and d == 2:
                    value = jnp.where(border, 0.0, value)
                c_ref[at : at + 8, :] = value

    def load(ref, t, count=parts):
        at = t * (count * 8)
        at = at if isinstance(at, int) else pl.multiple_of(at, 8)
        return [ref[pl.ds(at + 8 * i, 8), :] for i in range(count)]

    def save(ref, t, value):
        at = t * (parts * 8)
        at = at if isinstance(at, int) else pl.multiple_of(at, 8)
        for i in range(parts):
            ref[pl.ds(at + 8 * i, 8), :] = value[i]

    def update(previous, current, following, coefs, source):
        easts = current[1:] + [pltpu.roll(current[0], LANES - 1, 1)]
        wests = [pltpu.roll(current[-1], 1, 1)] + current[:-1]
        result = []
        for i in range(parts):
            ce, cw, co, ci = coefs[4 * i : 4 * i + 4]
            result.append(
                ((source[i] + co * previous[i]) + ci * following[i])
                + (ce * easts[i] + cw * wests[i])
            )
        return result

    unroll = min(UNROLL, seg)

    def march(from_ref, to_ref):
        x1 = load(from_ref, 0)
        x0 = [seam(v, True) for v in x1]
        save(from_ref, seg, [seam(v, False) for v in load(from_ref, seg - 1)])

        def rows_of(block, carry):
            x0, x1 = carry
            for i in range(unroll):
                t = block * unroll + i
                x2 = load(from_ref, t + 1)
                save(to_ref, t, update(x0, x1, x2, load(c_ref, t, 4 * parts), load(s_ref, t)))
                x0, x1 = x1, x2
            return x0, x1

        if seg == unroll:
            rows_of(0, (x0, x1))
        else:
            lax.fori_loop(0, seg // unroll, rows_of, (x0, x1))

    march(s_ref, xa_ref)

    def more(_, carry):
        march(xa_ref, xb_ref)
        march(xb_ref, xa_ref)
        return carry

    lax.fori_loop(0, SWEEPS // 2 - 1, more, 0)

    state = jnp.concatenate(
        [
            jnp.concatenate(
                [xa_ref[(t * parts + i) * 8 : (t * parts + i + 1) * 8, :] for t in range(seg)], axis=0
            ).astype(BF16)
            for i in range(parts)
        ],
        axis=1,
    )
    shape = (parts * LANES, wells * LANES)
    column, well = window_column(wells, shape, 0)
    dst = iota(shape, 1)
    order = one_hot((column == dst % LANES + HALO) & (well == dst // LANES))
    adjoints = dot(fold_rows(rows, True), dot(state, order).astype(BF16)).astype(BF16)
    mom_ref[...] = jnp.zeros(mom_ref.shape, F32)
    span = wells * rows // 2
    both = []
    for w in range(wells):
        adjoint = adjoints[:, w * LANES : (w + 1) * LANES]
        adj_refs[w // adj_refs[0].shape[0]][w % adj_refs[0].shape[0]] = adjoint
        both.append(lax.dot_general(
            basis_ref[...], adjoint, (((1,), (1,)), ((), ())), preferred_element_type=F32
        ))
        sampled = dot(adjoint, cw_ref[...]) * rw_ref[...]
        mom_ref[w : w + 1, span : span + LANES] = jnp.sum(sampled, axis=0, keepdims=True)
    both = jnp.concatenate(both, axis=1)
    both = both[0:4] + both[4:8]
    for h in range(2):
        mom_ref[4 * h : 4 * h + 4, :span] = both[:, h * span : (h + 1) * span]


def moment(mom_ref, index, which):
    span = mom_ref.shape[2] - LANES
    return jnp.concatenate(
        [mom_ref[index, which + 4 * h : which + 4 * h + 1, :span] for h in range(2)], axis=1
    )


def factor_kernel(place_ref, corr_ref, taper_ref, mats_ref, row_ref, spread_ref):
    rows = row_ref.shape[0]
    col, taper = place_ref[1], taper_ref[1]
    row_scale, row_reach, col_scale, col_reach = scales(corr_ref, taper_ref, rows)
    kind, c = iota((16, LANES), 0), iota((16, LANES), 1)
    near = jnp.where(kind % 4 < 2, c, LANES - 1 - c).astype(F32)
    spread = jnp.exp(-near / col_scale) * jnp.where(
        kind % 2 == 0, 1.0 - near / col_reach, -LANES / col_reach
    )
    high = spread.astype(BF16).astype(F32)
    spread = jnp.where(kind < 8, high, jnp.where(kind < 12, spread - high, 0.0))
    spread_ref[...] = spread.astype(BF16)
    src, dst = iota((LANES, LANES), 0), iota((LANES, LANES), 1)
    even = lax.rem(lax.div(col, taper), 2) == 0
    shift = jnp.where(even, taper, -taper) * LANES
    for i, away in enumerate((0, shift, -shift)):
        mats_ref[i] = factor(dst - src - away, col_scale, col_reach).astype(BF16)
    offset = iota((rows, rows), 0) - iota((rows, rows), 1)
    row_ref[...] = factor(offset, row_scale, row_reach).astype(BF16)


def moment_kernel(offsets, place_ref, corr_ref, taper_ref, mom_ref, mats_ref, spread_ref, *refs):
    half = len(refs) // 2
    adj_refs, out_refs = refs[:half], refs[half:]
    col, taper = place_ref[1], taper_ref[1]
    col_scale = corr_ref[1] * BLOCK
    scale_v = jnp.ones((1, LANES), F32) * col_scale
    per, rows, _ = adj_refs[0].shape
    span = half * per * rows
    sums = [jnp.zeros((1, span), F32) for _ in range(4)]
    for index, offset in enumerate(offsets):
        if offset == 0:
            continue
        away = lax.bitwise_xor(col, offset) - col
        for side, k in ((0, -away), (1, away)):
            live = (k >= 1) & (k < taper)
            gap = jnp.maximum(k - 1, 0).astype(F32)
            gain = jnp.where(live, 1.0, 0.0) * jnp.exp(-gap * LANES / scale_v)
            gain = gain[:, :1]
            zero = moment(mom_ref, index, 2 * side)
            one = moment(mom_ref, index, 2 * side + 1)
            sums[2 * side] = sums[2 * side] + gain * zero
            sums[2 * side + 1] = sums[2 * side + 1] + gain * (gap * zero + one)
    stacked = jnp.concatenate(sums * 4, axis=0)
    kind = iota((16, span), 0)
    high = stacked.astype(BF16).astype(F32)
    stacked = jnp.where((kind >= 4) & (kind < 8), stacked - high, high).astype(BF16)
    for w in range(half * per):
        base = lax.dot_general(
            stacked[:, w * rows : (w + 1) * rows], spread_ref[...],
            (((0,), (0,)), ((), ())), preferred_element_type=F32,
        )
        out_refs[w // per][w % per] = base + dot(adj_refs[w // per][w % per], mats_ref[0])


def mix_kernel(swapped, tiles, place_ref, base_ref, mats_ref, row_ref, *refs):
    out_refs = refs[tiles:]
    wells, rows, _ = base_ref.shape
    for w in range(wells):
        mixed = base_ref[w]
        for i in range(tiles):
            mixed = mixed + dot(refs[i][w], mats_ref[1 + i])
        field = dot(row_ref[...], mixed.astype(BF16)).astype(BF16)
        if swapped:
            half = rows // 2
            keep = place_ref[0] == 0
            out_refs[0][w] = jnp.where(keep, field[:half], field[half:])
            out_refs[1][w] = jnp.where(keep, field[half:], field[:half])
        else:
            out_refs[0][w] = field


VMEM = pl.BlockSpec(memory_space=pltpu.VMEM)
SMEM = pl.BlockSpec(memory_space=pltpu.SMEM)


def call(kernel, smem, vmem, outs, scratch=(), flops=1, whole=VMEM, limit=48 * 2**20):
    return pl.pallas_call(
        kernel,
        in_specs=[SMEM] * len(smem) + [whole] * len(vmem),
        out_specs=[VMEM] * len(outs),
        out_shape=[jax.ShapeDtypeStruct(shape, dtype) for shape, dtype in outs],
        scratch_shapes=list(scratch),
        compiler_params=pltpu.CompilerParams(vmem_limit_bytes=limit),
        cost_estimate=pl.CostEstimate(flops=flops, bytes_accessed=2**20, transcendentals=0),
    )(*smem, *vmem)


def pairs_at(count, distance, odd):
    pairs = []
    for i in range(count - distance):
        if (i // distance) % 2 == odd:
            pairs += [(i, i + distance), (i + distance, i)]
    return pairs


def exchanged(value, axis):
    return lax.ppermute(value, axis, [(0, 1), (1, 0)])


def local(log_trans, corr_len, taper_width, well_cells, obs_weight):
    tile_rows, tile_cols = log_trans.shape
    row_count, col_count = lax.axis_size("row"), lax.axis_size("col")
    total_rows, total_cols = tile_rows * row_count, tile_cols * col_count
    well_count = well_cells.shape[1]
    wells = well_count // row_count
    row, col = lax.axis_index("row"), lax.axis_index("col")
    place = jnp.stack([row, col]).astype(jnp.int32)
    own = obs_weight[0]
    swapped = row_count == 2
    tile = (wells, total_rows, tile_cols)

    if swapped:
        half = ((wells, tile_rows, tile_cols), BF16)
        sent, kept, planes = call(
            split_kernel, (place,), (own, log_trans),
            [half, half, ((3, tile_rows, tile_cols), BF16)],
            [pltpu.VMEM((tile_rows, tile_cols), F32), pltpu.SemaphoreType.DMA((3,))],
            whole=pl.BlockSpec(memory_space=pl.ANY),
        )
        operands = (kept, planes, exchanged(sent, "row"), exchanged(log_trans, "row"))
    else:
        operands = (
            lax.all_to_all(own, "row", 0, 1, tiled=True),
            lax.all_gather(log_trans, "row", axis=0, tiled=True),
        )
    packed = call(
        functools.partial(pack_kernel, swapped), (place,), operands,
        [((total_rows + total_rows // PACK, LANES), BF16)] * 2,
    )
    received = [
        lax.ppermute(value, "col", pairs_at(col_count, 1, odd)) for odd, value in enumerate(packed)
    ]
    parts = layout(wells)[1]
    placed = ((total_rows, parts * LANES), F32)
    prepared = call(
        functools.partial(own_kernel, swapped, wells, total_cols),
        (place, corr_len, taper_width, well_cells), operands,
        [placed, placed, ((8, LANES), BF16), ((total_rows, LANES), F32), ((LANES, LANES), BF16)],
        [pltpu.VMEM((total_rows, (wells + 3) * LANES), BF16)],
    )
    seg = total_rows // 8
    chunks = min(CHUNKS, wells)
    piece = (wells // chunks,) + tile[1:]
    *adjoints, moments = call(
        functools.partial(sweep_kernel, wells, tile_rows if swapped else total_rows, total_cols),
        (place,), (*prepared, *received),
        [(piece, BF16)] * chunks + [((8, wells * total_rows // 2 + LANES), F32)],
        [
            pltpu.VMEM(((seg + 1) * parts * 8, LANES), F32),
            pltpu.VMEM(((seg + 1) * parts * 8, LANES), F32),
            pltpu.VMEM(((seg + 1) * parts * 8, LANES), F32),
            pltpu.VMEM((seg * parts * 32, LANES), F32),
        ],
    )

    def finish(distance, moments, *adjoints):
        borders = [pairs_at(col_count, distance, odd) for odd in range(2)]
        borders = [pairs for pairs in borders if pairs]
        tiles = [[lax.ppermute(part, "col", pairs) for pairs in borders] for part in adjoints]
        mats, row_mix, spread = call(
            factor_kernel, (place, corr_len, taper_width), (),
            [((3, LANES, LANES), BF16), ((total_rows, total_rows), BF16), ((16, LANES), BF16)],
        )
        gathered, offsets = moments[None], [0]
        step = col_count // 2
        while step:
            moved = lax.ppermute(gathered, "col", [(i, i ^ step) for i in range(col_count)])
            gathered = jnp.concatenate([gathered, moved], axis=0)
            offsets = offsets + [offset ^ step for offset in offsets]
            step //= 2
        samples = [gathered[i, :wells, -LANES:] for i in range(col_count)]
        while len(samples) > 1:
            samples = [a + b for a, b in zip(samples[::2], samples[1::2])]
        samples = samples[0][:, : 2 * well_count]
        bases = call(
            functools.partial(moment_kernel, tuple(offsets)), (place, corr_len, taper_width),
            (gathered, mats, spread, *adjoints), [(piece, F32)] * chunks,
        )
        low, front = row == 0, lax.axis_index("sect") == 0
        if swapped:
            theirs = exchanged(samples, "row")
            samples = jnp.concatenate(
                [jnp.where(low, samples, theirs), jnp.where(low, theirs, samples)], axis=0
            )
        else:
            samples = lax.all_gather(samples, "row", axis=0, tiled=True)
        theirs = exchanged(samples, "sect")
        samples = jnp.concatenate(
            [jnp.where(front, samples, theirs), jnp.where(front, theirs, samples)], axis=0
        ).T
        half = (piece[0], tile_rows, tile_cols)
        kept, others = [], []
        for base, received in zip(bases, tiles):
            fields = call(
                functools.partial(mix_kernel, swapped, len(borders)), (place,),
                (base, mats, row_mix, *received),
                [(half, BF16)] * 2 if swapped else [(piece, BF16)],
            )
            kept.append(fields[0])
            if swapped:
                others.append(exchanged(fields[1], "row"))
        if swapped:
            qh_fields = jnp.concatenate(
                [jnp.where(low, a, b) for a, b in zip(kept, others)]
                + [jnp.where(low, b, a) for a, b in zip(kept, others)], axis=0
            )
        else:
            qh_fields = lax.all_to_all(jnp.concatenate(kept), "row", 1, 0, tiled=True)
        return qh_fields[None], samples

    branches = [functools.partial(finish, distance) for distance in range(1, TAPER + 1)]
    return lax.switch(taper_width[1] - 1, branches, moments, *adjoints)


def solution(mesh):
    placed = (P("row", "col"), P(), P(), P(), P("sect", None, "row", "col"))
    return jax.shard_map(
        local,
        mesh=mesh,
        in_specs=placed,
        out_specs=(P("sect", None, "row", "col"), P()),
        check_vma=False,
    )
```

```python
import functools

import jax
import jax.numpy as jnp
from jax import lax
from jax.experimental import pallas as pl
from jax.experimental.pallas import tpu as pltpu
from jax.sharding import PartitionSpec as P

BLOCK = 128
TAPER = 4
SWEEPS = 24
HALO = 24
LANES = 128
STRIP = 32
PACK = LANES // STRIP
CHUNKS = 1
UNROLL = 32

leakage = 0.05
F32, BF16 = jnp.float32, jnp.bfloat16


def iota(shape, dim):
    return lax.broadcasted_iota(jnp.int32, shape, dim)


def one_hot(mask):
    return jnp.where(mask, 1.0, 0.0).astype(BF16)


def dot(a, b):
    return jnp.dot(a, b, preferred_element_type=F32)


def harmonic(a, b):
    return 2.0 * a * b / (a + b)


def factor(offset, scale, reach):
    distance = jnp.abs(offset).astype(F32)
    return jnp.exp(-distance / scale) * jnp.maximum(1.0 - distance / reach, 0.0)


def scales(corr_ref, taper_ref, total_rows):
    row_scale = corr_ref[0] * (total_rows / 4.0)
    row_reach = (taper_ref[0] + TAPER).astype(F32) * (total_rows / (2.0 * TAPER)) + 1.0
    col_scale = corr_ref[1] * BLOCK
    col_reach = (taper_ref[1] * BLOCK + 1).astype(F32)
    return row_scale, row_reach, col_scale, col_reach


def split3(value):
    pieces = []
    for _ in range(3):
        piece = value.astype(BF16)
        pieces.append(piece)
        value = value - piece.astype(F32)
    return pieces


def strip_slot(lane, wells):
    slot, k = lane // HALO, lane % HALO
    return jnp.where(slot <= wells, slot, -1), k


def strips(place_ref, fields, logs):
    even = lax.rem(place_ref[1], 2) == 0
    tail = LANES - HALO
    start_a = jnp.where(even, tail, 0)
    rows = fields[0].shape[0]
    values = jnp.concatenate(fields + [logs[0]], axis=1)
    shape = (values.shape[1], 2 * LANES)
    src, dst = iota(shape, 0), iota(shape, 1)
    slot, k = strip_slot(dst % LANES, len(fields))
    start = jnp.where(dst < LANES, start_a, tail - start_a)
    first = dot(values, one_hot((slot == src // LANES) & (src % LANES == k + start)))
    shape = (LANES, 2 * LANES)
    src, dst = iota(shape, 0), iota(shape, 1)
    start = jnp.where(dst < LANES, start_a, tail - start_a)
    k = dst % STRIP
    wide = dot(logs[1], one_hot((src == k + start) & (k < HALO)))
    block = rows // PACK
    lane = iota((block, 2 * LANES), 1) % LANES // STRIP
    second = jnp.zeros((block, 2 * LANES), F32)
    for q in range(PACK):
        second = jnp.where(lane == q, wide[q * block : (q + 1) * block], second)
    return [
        (first[:, at : at + LANES].astype(BF16), second[:, at : at + LANES].astype(BF16))
        for at in (0, LANES)
    ]


def split_kernel(lt_ref, planes_ref):
    for i, piece in enumerate(split3(lt_ref[...])):
        planes_ref[i] = piece


def row_parts(swapped, place_ref, refs, rows):
    if not swapped:
        obs_ref, lt_ref = refs
        return [(pl.ds(0, rows), [obs_ref[w] for w in range(obs_ref.shape[0])], split3(lt_ref[...]))]
    kept_ref, planes_ref, recv_ref, lt_ref = refs
    half = rows // 2
    mine = pl.multiple_of(place_ref[0] * half, half)
    other = pl.multiple_of(half - mine, half)
    wells = kept_ref.shape[0]
    return [
        (pl.ds(mine, half), [kept_ref[w] for w in range(wells)], [planes_ref[i] for i in range(3)]),
        (pl.ds(other, half), [recv_ref[w] for w in range(wells)], split3(lt_ref[...])),
    ]


def pack_kernel(swapped, place_ref, *refs):
    out_refs = refs[-2:]
    rows = out_refs[0].shape[0] * PACK // (PACK + 1)
    for where, fields, logs in row_parts(swapped, place_ref, refs[:-2], rows):
        block = where.size // PACK
        after = pl.multiple_of(rows + lax.div(where.start, PACK), 8)
        for ref, (first, second) in zip(out_refs, strips(place_ref, fields, logs)):
            ref[where, :] = first
            ref[pl.ds(after, block), :] = second


def layout(wells):
    width = LANES // wells
    return width, -(-(LANES + 2 * HALO) // width)


def fold_rows(rows, transposed=False):
    at, row = iota((rows, rows), int(transposed)), iota((rows, rows), 1 - int(transposed))
    seg = rows // 8
    t, g = at // 8, at % 8
    return one_hot(row == jnp.where(g % 2 == 0, g * seg + t, (g + 1) * seg - 1 - t))


def window_column(wells, shape, dim):
    width, parts = layout(wells)
    lane = iota(shape, dim)
    return parts * (lane % width) + lane // LANES, (lane % LANES) // width


def own_kernel(swapped, wells, total_cols, place_ref, corr_ref, taper_ref, cells_ref, *refs):
    field_ref, log_ref, basis_ref, rw_ref, cw_ref, all_ref = refs[-6:]
    rows = field_ref.shape[0]
    parts = layout(wells)[1]
    for where, fields, logs in row_parts(swapped, place_ref, refs[:-6], rows):
        for i, value in enumerate(fields + logs):
            all_ref[where, i * LANES : (i + 1) * LANES] = value
    folded = dot(fold_rows(rows), all_ref[...]).astype(BF16)
    edge = wells * LANES
    shape = (edge, parts * LANES)
    column, well = window_column(wells, shape, 1)
    src = iota(shape, 0)
    pick = one_hot((column == src % LANES + HALO) & (well == src // LANES))
    field_ref[...] = dot(folded[:, :edge], pick)
    shape = (3 * LANES, parts * LANES)
    column, _ = window_column(wells, shape, 1)
    pick = one_hot(column == iota(shape, 0) % LANES + HALO)
    log_ref[...] = dot(folded[:, edge:], pick)
    col = place_ref[1]
    row_scale, row_reach, col_scale, col_reach = scales(corr_ref, taper_ref, rows)
    kind, c = iota((8, LANES), 0), iota((8, LANES), 1)
    reach = jnp.where(kind % 4 < 2, LANES - c, c + 1).astype(F32)
    basis = jnp.exp(-reach / col_scale) * jnp.where(kind % 2 == 0, 1.0, reach / LANES)
    high = basis.astype(BF16)
    basis_ref[...] = jnp.where(kind < 4, high.astype(F32), basis - high.astype(F32)).astype(BF16)
    m_lane = iota((1, LANES), 1)
    cell = jnp.full((1, LANES), -1, jnp.int32)
    batches, per_batch = cells_ref.shape
    for b in range(batches):
        for n in range(per_batch):
            cell = jnp.where(m_lane == b * per_batch + n, cells_ref[b, n], cell)
    cell_row, cell_col = lax.div(cell, total_cols), lax.rem(cell, total_cols)
    row_weight = factor(cell_row - iota((rows, LANES), 0), row_scale, row_reach)
    rw_ref[...] = row_weight.astype(BF16).astype(F32)
    cw_ref[...] = factor(
        cell_col - (col * LANES + iota((LANES, LANES), 0)), col_scale, col_reach
    ).astype(BF16)


def seam(value, outer):
    group = iota(value.shape, 0)
    up = pltpu.roll(value, 1, 0)
    down = pltpu.roll(value, 7, 0)
    return jnp.where((group % 2 == 0) == (not outer), down, up)


def sweep_kernel(wells, tile_rows, total_cols, place_ref, field_ref, log_ref, basis_ref, rw_ref,
                 cw_ref, a_ref, b_ref, *refs):
    adj_refs = refs[:-5]
    mom_ref, xa_ref, xb_ref, s_ref, c_ref = refs[-5:]
    rows = field_ref.shape[0]
    seg = rows // 8
    width, parts = layout(wells)
    col = place_ref[1]
    even = lax.rem(col, 2) == 0
    a, b = a_ref[...], b_ref[...]
    sides = []
    for side in (jnp.where(even, b, a), jnp.where(even, a, b)):
        block = tile_rows // PACK
        blank = jnp.zeros((block, LANES), BF16)
        quarter = iota((block, LANES), 1) // STRIP
        second = [
            jnp.where(quarter == q, side[rows + p * block : rows + (p + 1) * block], blank)
            for p in range(rows // tile_rows) for q in range(PACK)
        ]
        sides.append((side[:rows], jnp.concatenate(second, axis=0)))
    strip = jnp.concatenate([sides[0][0], sides[1][0], sides[0][1], sides[1][1]], axis=1)
    folded = dot(fold_rows(rows), strip).astype(BF16)
    shape = (2 * LANES, parts * LANES)
    column, well = window_column(wells, shape, 1)
    src = iota(shape, 0)
    base = jnp.where(src < LANES, 0, LANES + HALO)
    slot, k = strip_slot(src % LANES, wells)
    hit = column == k + base
    k = src % STRIP
    again = (k < HALO) & (column == k + base)
    fields = field_ref[...] + dot(folded[:, : 2 * LANES], one_hot(hit & (slot == well)))
    logs = log_ref[...] + dot(folded[:, : 2 * LANES], one_hot(hit & (slot == wells)))
    logs = logs + dot(folded[:, 2 * LANES :], one_hot(again))

    cond = jnp.exp(logs)
    cond = [cond[:, i * LANES : (i + 1) * LANES] for i in range(parts)]
    lane = iota((1, LANES), 1)
    group = iota((8, LANES), 0)
    border = (group == 0) | (group == 7)
    east = [harmonic(cond[i], cond[i + 1]) for i in range(parts - 1)]
    east.append(harmonic(cond[-1], pltpu.roll(cond[0], LANES - 1, 1)))
    west = [pltpu.roll(east[-1], 1, 1)] + east[:-1]
    for i in range(parts):
        place = parts * (lane % width) + i
        column = col * LANES - HALO + place
        inside = (column >= 0) & (column < total_cols) & (place < LANES + 2 * HALO)
        here = cond[i]
        inner = harmonic(here, jnp.concatenate([here[8:], seam(here[-8:], False)], axis=0))
        first = harmonic(here[:8], seam(here[:8], True))
        outer = jnp.concatenate([jnp.where(border, here[:8], first), inner[:-8]], axis=0)
        fe = jnp.where(column < total_cols - 1, east[i], here)
        fw = jnp.where(column > 0, west[i], here)
        inverse = jnp.where(inside, 1.0 / (fe + fw + outer + inner + leakage), 0.0)
        values = [fe * inverse, fw * inverse, outer * inverse, inner * inverse]
        source = fields[:, i * LANES : (i + 1) * LANES] * inverse
        for t in range(seg):
            s_ref[(t * parts + i) * 8 : (t * parts + i + 1) * 8, :] = source[8 * t : 8 * t + 8]
            for d in range(4):
                at = ((t * parts + i) * 4 + d) * 8
                value = values[d][8 * t : 8 * t + 8]
                if t == 0 and d == 2:
                    value = jnp.where(border, 0.0, value)
                c_ref[at : at + 8, :] = value

    def load(ref, t, count=parts):
        at = t * (count * 8)
        at = at if isinstance(at, int) else pl.multiple_of(at, 8)
        return [ref[pl.ds(at + 8 * i, 8), :] for i in range(count)]

    def save(ref, t, value):
        at = t * (parts * 8)
        at = at if isinstance(at, int) else pl.multiple_of(at, 8)
        for i in range(parts):
            ref[pl.ds(at + 8 * i, 8), :] = value[i]

    def update(previous, current, following, coefs, source):
        easts = current[1:] + [pltpu.roll(current[0], LANES - 1, 1)]
        wests = [pltpu.roll(current[-1], 1, 1)] + current[:-1]
        result = []
        for i in range(parts):
            ce, cw, co, ci = coefs[4 * i : 4 * i + 4]
            result.append(
                ((source[i] + co * previous[i]) + ci * following[i])
                + (ce * easts[i] + cw * wests[i])
            )
        return result

    unroll = min(UNROLL, seg)

    def march(from_ref, to_ref):
        x1 = load(from_ref, 0)
        x0 = [seam(v, True) for v in x1]
        save(from_ref, seg, [seam(v, False) for v in load(from_ref, seg - 1)])

        def rows_of(block, carry):
            x0, x1 = carry
            for i in range(unroll):
                t = block * unroll + i
                x2 = load(from_ref, t + 1)
                save(to_ref, t, update(x0, x1, x2, load(c_ref, t, 4 * parts), load(s_ref, t)))
                x0, x1 = x1, x2
            return x0, x1

        if seg == unroll:
            rows_of(0, (x0, x1))
        else:
            lax.fori_loop(0, seg // unroll, rows_of, (x0, x1))

    march(s_ref, xa_ref)

    def more(_, carry):
        march(xa_ref, xb_ref)
        march(xb_ref, xa_ref)
        return carry

    lax.fori_loop(0, SWEEPS // 2 - 1, more, 0)

    state = jnp.concatenate(
        [
            jnp.concatenate(
                [xa_ref[(t * parts + i) * 8 : (t * parts + i + 1) * 8, :] for t in range(seg)], axis=0
            ).astype(BF16)
            for i in range(parts)
        ],
        axis=1,
    )
    shape = (parts * LANES, wells * LANES)
    column, well = window_column(wells, shape, 0)
    dst = iota(shape, 1)
    order = one_hot((column == dst % LANES + HALO) & (well == dst // LANES))
    adjoints = dot(fold_rows(rows, True), dot(state, order).astype(BF16)).astype(BF16)
    mom_ref[...] = jnp.zeros(mom_ref.shape, F32)
    span = wells * rows // 2
    both = []
    for w in range(wells):
        adjoint = adjoints[:, w * LANES : (w + 1) * LANES]
        adj_refs[w // adj_refs[0].shape[0]][w % adj_refs[0].shape[0]] = adjoint
        both.append(lax.dot_general(
            basis_ref[...], adjoint, (((1,), (1,)), ((), ())), preferred_element_type=F32
        ))
        sampled = dot(adjoint, cw_ref[...]) * rw_ref[...]
        mom_ref[w : w + 1, span : span + LANES] = jnp.sum(sampled, axis=0, keepdims=True)
    both = jnp.concatenate(both, axis=1)
    both = both[0:4] + both[4:8]
    for h in range(2):
        mom_ref[4 * h : 4 * h + 4, :span] = both[:, h * span : (h + 1) * span]


def moment(mom_ref, index, which):
    span = mom_ref.shape[2] - LANES
    return jnp.concatenate(
        [mom_ref[index, which + 4 * h : which + 4 * h + 1, :span] for h in range(2)], axis=1
    )


def factor_kernel(place_ref, corr_ref, taper_ref, mats_ref, row_ref, spread_ref):
    rows = row_ref.shape[0]
    col, taper = place_ref[1], taper_ref[1]
    row_scale, row_reach, col_scale, col_reach = scales(corr_ref, taper_ref, rows)
    kind, c = iota((16, LANES), 0), iota((16, LANES), 1)
    near = jnp.where(kind % 4 < 2, c, LANES - 1 - c).astype(F32)
    spread = jnp.exp(-near / col_scale) * jnp.where(
        kind % 2 == 0, 1.0 - near / col_reach, -LANES / col_reach
    )
    high = spread.astype(BF16).astype(F32)
    spread = jnp.where(kind < 8, high, jnp.where(kind < 12, spread - high, 0.0))
    spread_ref[...] = spread.astype(BF16)
    src, dst = iota((LANES, LANES), 0), iota((LANES, LANES), 1)
    even = lax.rem(lax.div(col, taper), 2) == 0
    shift = jnp.where(even, taper, -taper) * LANES
    for i, away in enumerate((0, shift, -shift)):
        mats_ref[i] = factor(dst - src - away, col_scale, col_reach).astype(BF16)
    offset = iota((rows, rows), 0) - iota((rows, rows), 1)
    row_ref[...] = factor(offset, row_scale, row_reach).astype(BF16)


def moment_kernel(offsets, place_ref, corr_ref, taper_ref, mom_ref, mats_ref, spread_ref, *refs):
    half = len(refs) // 2
    adj_refs, out_refs = refs[:half], refs[half:]
    col, taper = place_ref[1], taper_ref[1]
    col_scale = corr_ref[1] * BLOCK
    scale_v = jnp.ones((1, LANES), F32) * col_scale
    per, rows, _ = adj_refs[0].shape
    span = half * per * rows
    sums = [jnp.zeros((1, span), F32) for _ in range(4)]
    for index, offset in enumerate(offsets):
        if offset == 0:
            continue
        away = lax.bitwise_xor(col, offset) - col
        for side, k in ((0, -away), (1, away)):
            live = (k >= 1) & (k < taper)
            gap = jnp.maximum(k - 1, 0).astype(F32)
            gain = jnp.where(live, 1.0, 0.0) * jnp.exp(-gap * LANES / scale_v)
            gain = gain[:, :1]
            zero = moment(mom_ref, index, 2 * side)
            one = moment(mom_ref, index, 2 * side + 1)
            sums[2 * side] = sums[2 * side] + gain * zero
            sums[2 * side + 1] = sums[2 * side + 1] + gain * (gap * zero + one)
    stacked = jnp.concatenate(sums * 4, axis=0)
    kind = iota((16, span), 0)
    high = stacked.astype(BF16).astype(F32)
    stacked = jnp.where((kind >= 4) & (kind < 8), stacked - high, high).astype(BF16)
    for w in range(half * per):
        base = lax.dot_general(
            stacked[:, w * rows : (w + 1) * rows], spread_ref[...],
            (((0,), (0,)), ((), ())), preferred_element_type=F32,
        )
        out_refs[w // per][w % per] = base + dot(adj_refs[w // per][w % per], mats_ref[0])


def mix_kernel(swapped, tiles, place_ref, base_ref, mats_ref, row_ref, *refs):
    out_refs = refs[tiles:]
    wells, rows, _ = base_ref.shape
    for w in range(wells):
        mixed = base_ref[w]
        for i in range(tiles):
            mixed = mixed + dot(refs[i][w], mats_ref[1 + i])
        field = dot(row_ref[...], mixed.astype(BF16)).astype(BF16)
        if swapped:
            half = rows // 2
            keep = place_ref[0] == 0
            out_refs[0][w] = jnp.where(keep, field[:half], field[half:])
            out_refs[1][w] = jnp.where(keep, field[half:], field[:half])
        else:
            out_refs[0][w] = field


VMEM = pl.BlockSpec(memory_space=pltpu.VMEM)
SMEM = pl.BlockSpec(memory_space=pltpu.SMEM)


def call(kernel, smem, vmem, outs, scratch=(), flops=1, whole=VMEM, limit=48 * 2**20):
    return pl.pallas_call(
        kernel,
        in_specs=[SMEM] * len(smem) + [whole] * len(vmem),
        out_specs=[VMEM] * len(outs),
        out_shape=[jax.ShapeDtypeStruct(shape, dtype) for shape, dtype in outs],
        scratch_shapes=list(scratch),
        compiler_params=pltpu.CompilerParams(vmem_limit_bytes=limit),
        cost_estimate=pl.CostEstimate(flops=flops, bytes_accessed=2**20, transcendentals=0),
    )(*smem, *vmem)


def pairs_at(count, distance, odd):
    pairs = []
    for i in range(count - distance):
        if (i // distance) % 2 == odd:
            pairs += [(i, i + distance), (i + distance, i)]
    return pairs


def exchanged(value, axis):
    return lax.ppermute(value, axis, [(0, 1), (1, 0)])


def local(log_trans, corr_len, taper_width, well_cells, obs_weight):
    tile_rows, tile_cols = log_trans.shape
    row_count, col_count = lax.axis_size("row"), lax.axis_size("col")
    total_rows, total_cols = tile_rows * row_count, tile_cols * col_count
    well_count = well_cells.shape[1]
    wells = well_count // row_count
    row, col = lax.axis_index("row"), lax.axis_index("col")
    place = jnp.stack([row, col]).astype(jnp.int32)
    own = obs_weight[0]
    swapped = row_count == 2
    tile = (wells, total_rows, tile_cols)

    if swapped:
        sent, kept = [
            lax.dynamic_slice_in_dim(own, first * wells, wells, axis=0) for first in (1 - row, row)
        ]
        (planes,) = call(
            split_kernel, (), (log_trans,), [((3, tile_rows, tile_cols), BF16)]
        )
        operands = (kept, planes, exchanged(sent, "row"), exchanged(log_trans, "row"))
    else:
        operands = (
            lax.all_to_all(own, "row", 0, 1, tiled=True),
            lax.all_gather(log_trans, "row", axis=0, tiled=True),
        )
    packed = call(
        functools.partial(pack_kernel, swapped), (place,), operands,
        [((total_rows + total_rows // PACK, LANES), BF16)] * 2,
    )
    received = [
        lax.ppermute(value, "col", pairs_at(col_count, 1, odd)) for odd, value in enumerate(packed)
    ]
    parts = layout(wells)[1]
    placed = ((total_rows, parts * LANES), F32)
    prepared = call(
        functools.partial(own_kernel, swapped, wells, total_cols),
        (place, corr_len, taper_width, well_cells), operands,
        [placed, placed, ((8, LANES), BF16), ((total_rows, LANES), F32), ((LANES, LANES), BF16)],
        [pltpu.VMEM((total_rows, (wells + 3) * LANES), BF16)],
    )
    seg = total_rows // 8
    chunks = min(CHUNKS, wells)
    piece = (wells // chunks,) + tile[1:]
    *adjoints, moments = call(
        functools.partial(sweep_kernel, wells, tile_rows if swapped else total_rows, total_cols),
        (place,), (*prepared, *received),
        [(piece, BF16)] * chunks + [((8, wells * total_rows // 2 + LANES), F32)],
        [
            pltpu.VMEM(((seg + 1) * parts * 8, LANES), F32),
            pltpu.VMEM(((seg + 1) * parts * 8, LANES), F32),
            pltpu.VMEM(((seg + 1) * parts * 8, LANES), F32),
            pltpu.VMEM((seg * parts * 32, LANES), F32),
        ],
    )

    def finish(distance, moments, *adjoints):
        borders = [pairs_at(col_count, distance, odd) for odd in range(2)]
        borders = [pairs for pairs in borders if pairs]
        tiles = [[lax.ppermute(part, "col", pairs) for pairs in borders] for part in adjoints]
        mats, row_mix, spread = call(
            factor_kernel, (place, corr_len, taper_width), (),
            [((3, LANES, LANES), BF16), ((total_rows, total_rows), BF16), ((16, LANES), BF16)],
        )
        gathered, offsets = moments[None], [0]
        step = col_count // 2
        while step:
            moved = lax.ppermute(gathered, "col", [(i, i ^ step) for i in range(col_count)])
            gathered = jnp.concatenate([gathered, moved], axis=0)
            offsets = offsets + [offset ^ step for offset in offsets]
            step //= 2
        samples = [gathered[i, :wells, -LANES:] for i in range(col_count)]
        while len(samples) > 1:
            samples = [a + b for a, b in zip(samples[::2], samples[1::2])]
        samples = samples[0][:, : 2 * well_count]
        bases = call(
            functools.partial(moment_kernel, tuple(offsets)), (place, corr_len, taper_width),
            (gathered, mats, spread, *adjoints), [(piece, F32)] * chunks,
        )
        low, front = row == 0, lax.axis_index("sect") == 0
        if swapped:
            theirs = exchanged(samples, "row")
            samples = jnp.concatenate(
                [jnp.where(low, samples, theirs), jnp.where(low, theirs, samples)], axis=0
            )
        else:
            samples = lax.all_gather(samples, "row", axis=0, tiled=True)
        theirs = exchanged(samples, "sect")
        samples = jnp.concatenate(
            [jnp.where(front, samples, theirs), jnp.where(front, theirs, samples)], axis=0
        ).T
        half = (piece[0], tile_rows, tile_cols)
        kept, others = [], []
        for base, received in zip(bases, tiles):
            fields = call(
                functools.partial(mix_kernel, swapped, len(borders)), (place,),
                (base, mats, row_mix, *received),
                [(half, BF16)] * 2 if swapped else [(piece, BF16)],
            )
            kept.append(fields[0])
            if swapped:
                others.append(exchanged(fields[1], "row"))
        if swapped:
            qh_fields = jnp.concatenate(
                [jnp.where(low, a, b) for a, b in zip(kept, others)]
                + [jnp.where(low, b, a) for a, b in zip(kept, others)], axis=0
            )
        else:
            qh_fields = lax.all_to_all(jnp.concatenate(kept), "row", 1, 0, tiled=True)
        return qh_fields[None], samples

    branches = [functools.partial(finish, distance) for distance in range(1, TAPER + 1)]
    return lax.switch(taper_width[1] - 1, branches, moments, *adjoints)


def solution(mesh):
    placed = (P("row", "col"), P(), P(), P(), P("sect", None, "row", "col"))
    return jax.shard_map(
        local,
        mesh=mesh,
        in_specs=placed,
        out_specs=(P("sect", None, "row", "col"), P()),
        check_vma=False,
    )
```

```python
import functools

import jax
import jax.numpy as jnp
from jax import lax
from jax.experimental import pallas as pl
from jax.experimental.pallas import tpu as pltpu
from jax.sharding import PartitionSpec as P

BLOCK = 128
TAPER = 4
SWEEPS = 24
HALO = 24
LANES = 128
STRIP = 32
PACK = LANES // STRIP
CHUNKS = 1
UNROLL = 32

leakage = 0.05
F32, BF16 = jnp.float32, jnp.bfloat16


def iota(shape, dim):
    return lax.broadcasted_iota(jnp.int32, shape, dim)


def one_hot(mask):
    return jnp.where(mask, 1.0, 0.0).astype(BF16)


def dot(a, b):
    return jnp.dot(a, b, preferred_element_type=F32)


def harmonic(a, b):
    return 2.0 * a * b / (a + b)


def factor(offset, scale, reach):
    distance = jnp.abs(offset).astype(F32)
    return jnp.exp(-distance / scale) * jnp.maximum(1.0 - distance / reach, 0.0)


def scales(corr_ref, taper_ref, total_rows):
    row_scale = corr_ref[0] * (total_rows / 4.0)
    row_reach = (taper_ref[0] + TAPER).astype(F32) * (total_rows / (2.0 * TAPER)) + 1.0
    col_scale = corr_ref[1] * BLOCK
    col_reach = (taper_ref[1] * BLOCK + 1).astype(F32)
    return row_scale, row_reach, col_scale, col_reach


def split3(value):
    pieces = []
    for _ in range(3):
        piece = value.astype(BF16)
        pieces.append(piece)
        value = value - piece.astype(F32)
    return pieces


def strip_slot(lane, wells):
    slot, k = lane // HALO, lane % HALO
    return jnp.where(slot <= wells, slot, -1), k


def strips(place_ref, fields, logs):
    even = lax.rem(place_ref[1], 2) == 0
    tail = LANES - HALO
    start_a = jnp.where(even, tail, 0)
    rows = fields[0].shape[0]
    values = jnp.concatenate(fields + [logs[0]], axis=1)
    shape = (values.shape[1], 2 * LANES)
    src, dst = iota(shape, 0), iota(shape, 1)
    slot, k = strip_slot(dst % LANES, len(fields))
    start = jnp.where(dst < LANES, start_a, tail - start_a)
    first = dot(values, one_hot((slot == src // LANES) & (src % LANES == k + start)))
    shape = (LANES, 2 * LANES)
    src, dst = iota(shape, 0), iota(shape, 1)
    start = jnp.where(dst < LANES, start_a, tail - start_a)
    k = dst % STRIP
    wide = dot(logs[1], one_hot((src == k + start) & (k < HALO)))
    block = rows // PACK
    lane = iota((block, 2 * LANES), 1) % LANES // STRIP
    second = jnp.zeros((block, 2 * LANES), F32)
    for q in range(PACK):
        second = jnp.where(lane == q, wide[q * block : (q + 1) * block], second)
    return [
        (first[:, at : at + LANES].astype(BF16), second[:, at : at + LANES].astype(BF16))
        for at in (0, LANES)
    ]


def split_kernel(lt_ref, planes_ref):
    for i, piece in enumerate(split3(lt_ref[...])):
        planes_ref[i] = piece


def row_parts(swapped, place_ref, refs, rows):
    if not swapped:
        obs_ref, lt_ref = refs
        return [(pl.ds(0, rows), [obs_ref[w] for w in range(obs_ref.shape[0])], split3(lt_ref[...]))]
    kept_ref, planes_ref, recv_ref, lt_ref = refs
    half = rows // 2
    mine = pl.multiple_of(place_ref[0] * half, half)
    other = pl.multiple_of(half - mine, half)
    wells = kept_ref.shape[0]
    return [
        (pl.ds(mine, half), [kept_ref[w] for w in range(wells)], [planes_ref[i] for i in range(3)]),
        (pl.ds(other, half), [recv_ref[w] for w in range(wells)], split3(lt_ref[...])),
    ]


def pack_kernel(swapped, place_ref, *refs):
    out_refs = refs[-2:]
    rows = out_refs[0].shape[0] * PACK // (PACK + 1)
    for where, fields, logs in row_parts(swapped, place_ref, refs[:-2], rows):
        block = where.size // PACK
        after = pl.multiple_of(rows + lax.div(where.start, PACK), 8)
        for ref, (first, second) in zip(out_refs, strips(place_ref, fields, logs)):
            ref[where, :] = first
            ref[pl.ds(after, block), :] = second


def layout(wells):
    width = LANES // wells
    return width, -(-(LANES + 2 * HALO) // width)


def fold_rows(rows, transposed=False):
    at, row = iota((rows, rows), int(transposed)), iota((rows, rows), 1 - int(transposed))
    seg = rows // 8
    t, g = at // 8, at % 8
    return one_hot(row == jnp.where(g % 2 == 0, g * seg + t, (g + 1) * seg - 1 - t))


def window_column(wells, shape, dim):
    width, parts = layout(wells)
    lane = iota(shape, dim)
    return parts * (lane % width) + lane // LANES, (lane % LANES) // width


def own_kernel(swapped, wells, total_cols, place_ref, corr_ref, taper_ref, cells_ref, *refs):
    field_ref, log_ref, basis_ref, rw_ref, cw_ref, all_ref = refs[-6:]
    rows = field_ref.shape[0]
    parts = layout(wells)[1]
    for where, fields, logs in row_parts(swapped, place_ref, refs[:-6], rows):
        for i, value in enumerate(fields + logs):
            all_ref[where, i * LANES : (i + 1) * LANES] = value
    folded = dot(fold_rows(rows), all_ref[...]).astype(BF16)
    edge = wells * LANES
    shape = (edge, parts * LANES)
    column, well = window_column(wells, shape, 1)
    src = iota(shape, 0)
    pick = one_hot((column == src % LANES + HALO) & (well == src // LANES))
    field_ref[...] = dot(folded[:, :edge], pick)
    shape = (3 * LANES, parts * LANES)
    column, _ = window_column(wells, shape, 1)
    pick = one_hot(column == iota(shape, 0) % LANES + HALO)
    log_ref[...] = dot(folded[:, edge:], pick)
    col = place_ref[1]
    row_scale, row_reach, col_scale, col_reach = scales(corr_ref, taper_ref, rows)
    kind, c = iota((8, LANES), 0), iota((8, LANES), 1)
    reach = jnp.where(kind % 4 < 2, LANES - c, c + 1).astype(F32)
    basis = jnp.exp(-reach / col_scale) * jnp.where(kind % 2 == 0, 1.0, reach / LANES)
    high = basis.astype(BF16)
    basis_ref[...] = jnp.where(kind < 4, high.astype(F32), basis - high.astype(F32)).astype(BF16)
    m_lane = iota((1, LANES), 1)
    cell = jnp.full((1, LANES), -1, jnp.int32)
    batches, per_batch = cells_ref.shape
    for b in range(batches):
        for n in range(per_batch):
            cell = jnp.where(m_lane == b * per_batch + n, cells_ref[b, n], cell)
    cell_row, cell_col = lax.div(cell, total_cols), lax.rem(cell, total_cols)
    row_weight = factor(cell_row - iota((rows, LANES), 0), row_scale, row_reach)
    rw_ref[...] = row_weight.astype(BF16).astype(F32)
    cw_ref[...] = factor(
        cell_col - (col * LANES + iota((LANES, LANES), 0)), col_scale, col_reach
    ).astype(BF16)


def seam(value, outer):
    group = iota(value.shape, 0)
    up = pltpu.roll(value, 1, 0)
    down = pltpu.roll(value, 7, 0)
    return jnp.where((group % 2 == 0) == (not outer), down, up)


def sweep_kernel(wells, tile_rows, total_cols, place_ref, field_ref, log_ref, basis_ref, rw_ref,
                 cw_ref, a_ref, b_ref, *refs):
    adj_refs = refs[:-5]
    mom_ref, xa_ref, xb_ref, s_ref, c_ref = refs[-5:]
    rows = field_ref.shape[0]
    seg = rows // 8
    width, parts = layout(wells)
    col = place_ref[1]
    even = lax.rem(col, 2) == 0
    a, b = a_ref[...], b_ref[...]
    sides = []
    for side in (jnp.where(even, b, a), jnp.where(even, a, b)):
        block = tile_rows // PACK
        blank = jnp.zeros((block, LANES), BF16)
        quarter = iota((block, LANES), 1) // STRIP
        second = [
            jnp.where(quarter == q, side[rows + p * block : rows + (p + 1) * block], blank)
            for p in range(rows // tile_rows) for q in range(PACK)
        ]
        sides.append((side[:rows], jnp.concatenate(second, axis=0)))
    strip = jnp.concatenate([sides[0][0], sides[1][0], sides[0][1], sides[1][1]], axis=1)
    folded = dot(fold_rows(rows), strip).astype(BF16)
    shape = (2 * LANES, parts * LANES)
    column, well = window_column(wells, shape, 1)
    src = iota(shape, 0)
    base = jnp.where(src < LANES, 0, LANES + HALO)
    slot, k = strip_slot(src % LANES, wells)
    hit = column == k + base
    k = src % STRIP
    again = (k < HALO) & (column == k + base)
    fields = field_ref[...] + dot(folded[:, : 2 * LANES], one_hot(hit & (slot == well)))
    logs = log_ref[...] + dot(folded[:, : 2 * LANES], one_hot(hit & (slot == wells)))
    logs = logs + dot(folded[:, 2 * LANES :], one_hot(again))

    cond = jnp.exp(logs)
    cond = [cond[:, i * LANES : (i + 1) * LANES] for i in range(parts)]
    lane = iota((1, LANES), 1)
    group = iota((8, LANES), 0)
    border = (group == 0) | (group == 7)
    east = [harmonic(cond[i], cond[i + 1]) for i in range(parts - 1)]
    east.append(harmonic(cond[-1], pltpu.roll(cond[0], LANES - 1, 1)))
    west = [pltpu.roll(east[-1], 1, 1)] + east[:-1]
    for i in range(parts):
        place = parts * (lane % width) + i
        column = col * LANES - HALO + place
        inside = (column >= 0) & (column < total_cols) & (place < LANES + 2 * HALO)
        here = cond[i]
        inner = harmonic(here, jnp.concatenate([here[8:], seam(here[-8:], False)], axis=0))
        first = harmonic(here[:8], seam(here[:8], True))
        outer = jnp.concatenate([jnp.where(border, here[:8], first), inner[:-8]], axis=0)
        fe = jnp.where(column < total_cols - 1, east[i], here)
        fw = jnp.where(column > 0, west[i], here)
        inverse = jnp.where(inside, 1.0 / (fe + fw + outer + inner + leakage), 0.0)
        values = [fe * inverse, fw * inverse, outer * inverse, inner * inverse]
        source = fields[:, i * LANES : (i + 1) * LANES] * inverse
        for t in range(seg):
            s_ref[(t * parts + i) * 8 : (t * parts + i + 1) * 8, :] = source[8 * t : 8 * t + 8]
            for d in range(4):
                at = ((t * parts + i) * 4 + d) * 8
                value = values[d][8 * t : 8 * t + 8]
                if t == 0 and d == 2:
                    value = jnp.where(border, 0.0, value)
                c_ref[at : at + 8, :] = value

    def load(ref, t, count=parts):
        at = t * (count * 8)
        at = at if isinstance(at, int) else pl.multiple_of(at, 8)
        return [ref[pl.ds(at + 8 * i, 8), :] for i in range(count)]

    def save(ref, t, value):
        at = t * (parts * 8)
        at = at if isinstance(at, int) else pl.multiple_of(at, 8)
        for i in range(parts):
            ref[pl.ds(at + 8 * i, 8), :] = value[i]

    def update(previous, current, following, coefs, source):
        easts = current[1:] + [pltpu.roll(current[0], LANES - 1, 1)]
        wests = [pltpu.roll(current[-1], 1, 1)] + current[:-1]
        result = []
        for i in range(parts):
            ce, cw, co, ci = coefs[4 * i : 4 * i + 4]
            result.append(
                ((source[i] + co * previous[i]) + ci * following[i])
                + (ce * easts[i] + cw * wests[i])
            )
        return result

    unroll = min(UNROLL, seg)

    def march(from_ref, to_ref):
        x1 = load(from_ref, 0)
        x0 = [seam(v, True) for v in x1]
        save(from_ref, seg, [seam(v, False) for v in load(from_ref, seg - 1)])

        def rows_of(block, carry):
            x0, x1 = carry
            for i in range(unroll):
                t = block * unroll + i
                x2 = load(from_ref, t + 1)
                save(to_ref, t, update(x0, x1, x2, load(c_ref, t, 4 * parts), load(s_ref, t)))
                x0, x1 = x1, x2
            return x0, x1

        if seg == unroll:
            rows_of(0, (x0, x1))
        else:
            lax.fori_loop(0, seg // unroll, rows_of, (x0, x1))

    march(s_ref, xa_ref)

    def more(_, carry):
        march(xa_ref, xb_ref)
        march(xb_ref, xa_ref)
        return carry

    lax.fori_loop(0, SWEEPS // 2 - 1, more, 0)

    state = jnp.concatenate(
        [
            jnp.concatenate(
                [xa_ref[(t * parts + i) * 8 : (t * parts + i + 1) * 8, :] for t in range(seg)], axis=0
            ).astype(BF16)
            for i in range(parts)
        ],
        axis=1,
    )
    shape = (parts * LANES, wells * LANES)
    column, well = window_column(wells, shape, 0)
    dst = iota(shape, 1)
    order = one_hot((column == dst % LANES + HALO) & (well == dst // LANES))
    adjoints = dot(fold_rows(rows, True), dot(state, order).astype(BF16)).astype(BF16)
    mom_ref[...] = jnp.zeros(mom_ref.shape, F32)
    span = wells * rows // 2
    both = []
    for w in range(wells):
        adjoint = adjoints[:, w * LANES : (w + 1) * LANES]
        adj_refs[w // adj_refs[0].shape[0]][w % adj_refs[0].shape[0]] = adjoint
        both.append(lax.dot_general(
            basis_ref[...], adjoint, (((1,), (1,)), ((), ())), preferred_element_type=F32
        ))
        sampled = dot(adjoint, cw_ref[...]) * rw_ref[...]
        mom_ref[w : w + 1, span : span + LANES] = jnp.sum(sampled, axis=0, keepdims=True)
    both = jnp.concatenate(both, axis=1)
    both = both[0:4] + both[4:8]
    for h in range(2):
        mom_ref[4 * h : 4 * h + 4, :span] = both[:, h * span : (h + 1) * span]


def moment(mom_ref, index, which):
    span = mom_ref.shape[2] - LANES
    return jnp.concatenate(
        [mom_ref[index, which + 4 * h : which + 4 * h + 1, :span] for h in range(2)], axis=1
    )


def factor_kernel(place_ref, corr_ref, taper_ref, mats_ref, row_ref, spread_ref):
    rows = row_ref.shape[0]
    col, taper = place_ref[1], taper_ref[1]
    row_scale, row_reach, col_scale, col_reach = scales(corr_ref, taper_ref, rows)
    kind, c = iota((16, LANES), 0), iota((16, LANES), 1)
    near = jnp.where(kind % 4 < 2, c, LANES - 1 - c).astype(F32)
    spread = jnp.exp(-near / col_scale) * jnp.where(
        kind % 2 == 0, 1.0 - near / col_reach, -LANES / col_reach
    )
    high = spread.astype(BF16).astype(F32)
    spread = jnp.where(kind < 8, high, jnp.where(kind < 12, spread - high, 0.0))
    spread_ref[...] = spread.astype(BF16)
    src, dst = iota((LANES, LANES), 0), iota((LANES, LANES), 1)
    even = lax.rem(lax.div(col, taper), 2) == 0
    shift = jnp.where(even, taper, -taper) * LANES
    for i, away in enumerate((0, shift, -shift)):
        mats_ref[i] = factor(dst - src - away, col_scale, col_reach).astype(BF16)
    offset = iota((rows, rows), 0) - iota((rows, rows), 1)
    row_ref[...] = factor(offset, row_scale, row_reach).astype(BF16)


def moment_kernel(offsets, place_ref, corr_ref, taper_ref, mom_ref, mats_ref, spread_ref, *refs):
    half = len(refs) // 2
    adj_refs, out_refs = refs[:half], refs[half:]
    col, taper = place_ref[1], taper_ref[1]
    col_scale = corr_ref[1] * BLOCK
    scale_v = jnp.ones((1, LANES), F32) * col_scale
    per, rows, _ = adj_refs[0].shape
    span = half * per * rows
    sums = [jnp.zeros((1, span), F32) for _ in range(4)]
    for index, offset in enumerate(offsets):
        if offset == 0:
            continue
        away = lax.bitwise_xor(col, offset) - col
        for side, k in ((0, -away), (1, away)):
            live = (k >= 1) & (k < taper)
            gap = jnp.maximum(k - 1, 0).astype(F32)
            gain = jnp.where(live, 1.0, 0.0) * jnp.exp(-gap * LANES / scale_v)
            gain = gain[:, :1]
            zero = moment(mom_ref, index, 2 * side)
            one = moment(mom_ref, index, 2 * side + 1)
            sums[2 * side] = sums[2 * side] + gain * zero
            sums[2 * side + 1] = sums[2 * side + 1] + gain * (gap * zero + one)
    stacked = jnp.concatenate(sums * 4, axis=0)
    kind = iota((16, span), 0)
    high = stacked.astype(BF16).astype(F32)
    stacked = jnp.where((kind >= 4) & (kind < 8), stacked - high, high).astype(BF16)
    for w in range(half * per):
        base = lax.dot_general(
            stacked[:, w * rows : (w + 1) * rows], spread_ref[...],
            (((0,), (0,)), ((), ())), preferred_element_type=F32,
        )
        out_refs[w // per][w % per] = base + dot(adj_refs[w // per][w % per], mats_ref[0])


def mix_kernel(swapped, tiles, place_ref, base_ref, mats_ref, row_ref, *refs):
    out_refs = refs[tiles:]
    wells, rows, _ = base_ref.shape
    for w in range(wells):
        mixed = base_ref[w]
        for i in range(tiles):
            mixed = mixed + dot(refs[i][w], mats_ref[1 + i])
        field = dot(row_ref[...], mixed.astype(BF16)).astype(BF16)
        if swapped:
            half = rows // 2
            keep = place_ref[0] == 0
            out_refs[0][w] = jnp.where(keep, field[:half], field[half:])
            out_refs[1][w] = jnp.where(keep, field[half:], field[:half])
        else:
            out_refs[0][w] = field


VMEM = pl.BlockSpec(memory_space=pltpu.VMEM)
SMEM = pl.BlockSpec(memory_space=pltpu.SMEM)


def call(kernel, smem, vmem, outs, scratch=(), flops=1, whole=VMEM, limit=48 * 2**20):
    return pl.pallas_call(
        kernel,
        in_specs=[SMEM] * len(smem) + [whole] * len(vmem),
        out_specs=[VMEM] * len(outs),
        out_shape=[jax.ShapeDtypeStruct(shape, dtype) for shape, dtype in outs],
        scratch_shapes=list(scratch),
        compiler_params=pltpu.CompilerParams(vmem_limit_bytes=limit),
        cost_estimate=pl.CostEstimate(flops=flops, bytes_accessed=2**20, transcendentals=0),
    )(*smem, *vmem)


def pairs_at(count, distance, odd):
    pairs = []
    for i in range(count - distance):
        if (i // distance) % 2 == odd:
            pairs += [(i, i + distance), (i + distance, i)]
    return pairs


def exchanged(value, axis):
    return lax.ppermute(value, axis, [(0, 1), (1, 0)])


def local(log_trans, corr_len, taper_width, well_cells, obs_weight):
    tile_rows, tile_cols = log_trans.shape
    row_count, col_count = lax.axis_size("row"), lax.axis_size("col")
    total_rows, total_cols = tile_rows * row_count, tile_cols * col_count
    well_count = well_cells.shape[1]
    wells = well_count // row_count
    row, col = lax.axis_index("row"), lax.axis_index("col")
    place = jnp.stack([row, col]).astype(jnp.int32)
    own = obs_weight[0]
    swapped = row_count == 2
    tile = (wells, total_rows, tile_cols)

    if swapped:
        sent, kept = [
            lax.dynamic_slice_in_dim(own, first * wells, wells, axis=0) for first in (1 - row, row)
        ]
        (planes,) = call(
            split_kernel, (), (log_trans,), [((3, tile_rows, tile_cols), BF16)]
        )
        operands = (kept, planes, exchanged(sent, "row"), exchanged(log_trans, "row"))
    else:
        operands = (
            lax.all_to_all(own, "row", 0, 1, tiled=True),
            lax.all_gather(log_trans, "row", axis=0, tiled=True),
        )
    packed = call(
        functools.partial(pack_kernel, swapped), (place,), operands,
        [((total_rows + total_rows // PACK, LANES), BF16)] * 2,
    )
    received = [
        lax.ppermute(value, "col", pairs_at(col_count, 1, odd)) for odd, value in enumerate(packed)
    ]
    parts = layout(wells)[1]
    placed = ((total_rows, parts * LANES), F32)
    prepared = call(
        functools.partial(own_kernel, swapped, wells, total_cols),
        (place, corr_len, taper_width, well_cells), operands,
        [placed, placed, ((8, LANES), BF16), ((total_rows, LANES), F32), ((LANES, LANES), BF16)],
        [pltpu.VMEM((total_rows, (wells + 3) * LANES), BF16)],
    )
    seg = total_rows // 8
    chunks = min(CHUNKS, wells)
    piece = (wells // chunks,) + tile[1:]
    *adjoints, moments = call(
        functools.partial(sweep_kernel, wells, tile_rows if swapped else total_rows, total_cols),
        (place,), (*prepared, *received),
        [(piece, BF16)] * chunks + [((8, wells * total_rows // 2 + LANES), F32)],
        [
            pltpu.VMEM(((seg + 1) * parts * 8, LANES), F32),
            pltpu.VMEM(((seg + 1) * parts * 8, LANES), F32),
            pltpu.VMEM(((seg + 1) * parts * 8, LANES), F32),
            pltpu.VMEM((seg * parts * 32, LANES), F32),
        ],
    )

    def finish(distance, moments, *adjoints):
        borders = [pairs_at(col_count, distance, odd) for odd in range(2)]
        borders = [pairs for pairs in borders if pairs]
        tiles = [[lax.ppermute(part, "col", pairs) for pairs in borders] for part in adjoints]
        mats, row_mix, spread = call(
            factor_kernel, (place, corr_len, taper_width), (),
            [((3, LANES, LANES), BF16), ((total_rows, total_rows), BF16), ((16, LANES), BF16)],
        )
        gathered, offsets = moments[None], [0]
        steps = [1 << i for i in range(col_count.bit_length() - 1)][::-1]
        if distance == 3:
            steps[-2:] = steps[:-3:-1]
        for step in steps:
            moved = lax.ppermute(gathered, "col", [(i, i ^ step) for i in range(col_count)])
            gathered = jnp.concatenate([gathered, moved], axis=0)
            offsets = offsets + [offset ^ step for offset in offsets]
        samples = [gathered[i, :wells, -LANES:] for i in range(col_count)]
        while len(samples) > 1:
            samples = [a + b for a, b in zip(samples[::2], samples[1::2])]
        samples = samples[0][:, : 2 * well_count]
        bases = call(
            functools.partial(moment_kernel, tuple(offsets)), (place, corr_len, taper_width),
            (gathered, mats, spread, *adjoints), [(piece, F32)] * chunks,
        )
        low, front = row == 0, lax.axis_index("sect") == 0
        if swapped:
            theirs = exchanged(samples, "row")
            samples = jnp.concatenate(
                [jnp.where(low, samples, theirs), jnp.where(low, theirs, samples)], axis=0
            )
        else:
            samples = lax.all_gather(samples, "row", axis=0, tiled=True)
        theirs = exchanged(samples, "sect")
        samples = jnp.concatenate(
            [jnp.where(front, samples, theirs), jnp.where(front, theirs, samples)], axis=0
        ).T
        half = (piece[0], tile_rows, tile_cols)
        kept, others = [], []
        for base, received in zip(bases, tiles):
            fields = call(
                functools.partial(mix_kernel, swapped, len(borders)), (place,),
                (base, mats, row_mix, *received),
                [(half, BF16)] * 2 if swapped else [(piece, BF16)],
            )
            kept.append(fields[0])
            if swapped:
                others.append(exchanged(fields[1], "row"))
        if swapped:
            qh_fields = jnp.concatenate(
                [jnp.where(low, a, b) for a, b in zip(kept, others)]
                + [jnp.where(low, b, a) for a, b in zip(kept, others)], axis=0
            )
        else:
            qh_fields = lax.all_to_all(jnp.concatenate(kept), "row", 1, 0, tiled=True)
        return qh_fields[None], samples

    branches = [functools.partial(finish, distance) for distance in range(1, TAPER + 1)]
    return lax.switch(taper_width[1] - 1, branches, moments, *adjoints)


def solution(mesh):
    placed = (P("row", "col"), P(), P(), P(), P("sect", None, "row", "col"))
    return jax.shard_map(
        local,
        mesh=mesh,
        in_specs=placed,
        out_specs=(P("sect", None, "row", "col"), P()),
        check_vma=False,
    )
```

```python
import functools

import jax
import jax.numpy as jnp
from jax import lax
from jax.experimental import pallas as pl
from jax.experimental.pallas import tpu as pltpu
from jax.sharding import PartitionSpec as P

BLOCK = 128
TAPER = 4
SWEEPS = 24
HALO = 24
LANES = 128
STRIP = 32
PACK = LANES // STRIP
CHUNKS = 1
UNROLL = 32

leakage = 0.05
F32, BF16 = jnp.float32, jnp.bfloat16


def iota(shape, dim):
    return lax.broadcasted_iota(jnp.int32, shape, dim)


def one_hot(mask):
    return jnp.where(mask, 1.0, 0.0).astype(BF16)


def dot(a, b):
    return jnp.dot(a, b, preferred_element_type=F32)


def harmonic(a, b):
    return 2.0 * a * b / (a + b)


def factor(offset, scale, reach):
    distance = jnp.abs(offset).astype(F32)
    return jnp.exp(-distance / scale) * jnp.maximum(1.0 - distance / reach, 0.0)


def scales(corr_ref, taper_ref, total_rows):
    row_scale = corr_ref[0] * (total_rows / 4.0)
    row_reach = (taper_ref[0] + TAPER).astype(F32) * (total_rows / (2.0 * TAPER)) + 1.0
    col_scale = corr_ref[1] * BLOCK
    col_reach = (taper_ref[1] * BLOCK + 1).astype(F32)
    return row_scale, row_reach, col_scale, col_reach


def split3(value):
    pieces = []
    for _ in range(3):
        piece = value.astype(BF16)
        pieces.append(piece)
        value = value - piece.astype(F32)
    return pieces


def strip_slot(lane, wells):
    slot, k = lane // HALO, lane % HALO
    return jnp.where(slot <= wells, slot, -1), k


def strips(place_ref, fields, logs):
    even = lax.rem(place_ref[1], 2) == 0
    tail = LANES - HALO
    start_a = jnp.where(even, tail, 0)
    rows = fields[0].shape[0]
    values = jnp.concatenate(fields + [logs[0]], axis=1)
    shape = (values.shape[1], 2 * LANES)
    src, dst = iota(shape, 0), iota(shape, 1)
    slot, k = strip_slot(dst % LANES, len(fields))
    start = jnp.where(dst < LANES, start_a, tail - start_a)
    first = dot(values, one_hot((slot == src // LANES) & (src % LANES == k + start)))
    shape = (LANES, 2 * LANES)
    src, dst = iota(shape, 0), iota(shape, 1)
    start = jnp.where(dst < LANES, start_a, tail - start_a)
    k = dst % STRIP
    wide = dot(logs[1], one_hot((src == k + start) & (k < HALO)))
    block = rows // PACK
    lane = iota((block, 2 * LANES), 1) % LANES // STRIP
    second = jnp.zeros((block, 2 * LANES), F32)
    for q in range(PACK):
        second = jnp.where(lane == q, wide[q * block : (q + 1) * block], second)
    return [
        (first[:, at : at + LANES].astype(BF16), second[:, at : at + LANES].astype(BF16))
        for at in (0, LANES)
    ]


def split_kernel(lt_ref, planes_ref):
    for i, piece in enumerate(split3(lt_ref[...])):
        planes_ref[i] = piece


def row_parts(swapped, place_ref, refs, rows):
    if not swapped:
        obs_ref, lt_ref = refs
        return [(pl.ds(0, rows), [obs_ref[w] for w in range(obs_ref.shape[0])], split3(lt_ref[...]))]
    kept_ref, planes_ref, recv_ref, lt_ref = refs
    half = rows // 2
    mine = pl.multiple_of(place_ref[0] * half, half)
    other = pl.multiple_of(half - mine, half)
    wells = kept_ref.shape[0]
    return [
        (pl.ds(mine, half), [kept_ref[w] for w in range(wells)], [planes_ref[i] for i in range(3)]),
        (pl.ds(other, half), [recv_ref[w] for w in range(wells)], split3(lt_ref[...])),
    ]


def pack_kernel(swapped, place_ref, *refs):
    out_refs = refs[-2:]
    rows = out_refs[0].shape[0] * PACK // (PACK + 1)
    for where, fields, logs in row_parts(swapped, place_ref, refs[:-2], rows):
        block = where.size // PACK
        after = pl.multiple_of(rows + lax.div(where.start, PACK), 8)
        for ref, (first, second) in zip(out_refs, strips(place_ref, fields, logs)):
            ref[where, :] = first
            ref[pl.ds(after, block), :] = second


def layout(wells):
    width = LANES // wells
    return width, -(-(LANES + 2 * HALO) // width)


def fold_rows(rows, transposed=False):
    at, row = iota((rows, rows), int(transposed)), iota((rows, rows), 1 - int(transposed))
    seg = rows // 8
    t, g = at // 8, at % 8
    return one_hot(row == jnp.where(g % 2 == 0, g * seg + t, (g + 1) * seg - 1 - t))


def window_column(wells, shape, dim):
    width, parts = layout(wells)
    lane = iota(shape, dim)
    return parts * (lane % width) + lane // LANES, (lane % LANES) // width


def own_kernel(swapped, wells, total_cols, place_ref, corr_ref, taper_ref, cells_ref, *refs):
    field_ref, log_ref, basis_ref, rw_ref, cw_ref, all_ref = refs[-6:]
    rows = field_ref.shape[0]
    parts = layout(wells)[1]
    for where, fields, logs in row_parts(swapped, place_ref, refs[:-6], rows):
        for i, value in enumerate(fields + logs):
            all_ref[where, i * LANES : (i + 1) * LANES] = value
    folded = dot(fold_rows(rows), all_ref[...]).astype(BF16)
    edge = wells * LANES
    shape = (edge, parts * LANES)
    column, well = window_column(wells, shape, 1)
    src = iota(shape, 0)
    pick = one_hot((column == src % LANES + HALO) & (well == src // LANES))
    field_ref[...] = dot(folded[:, :edge], pick)
    shape = (3 * LANES, parts * LANES)
    column, _ = window_column(wells, shape, 1)
    pick = one_hot(column == iota(shape, 0) % LANES + HALO)
    log_ref[...] = dot(folded[:, edge:], pick)
    col = place_ref[1]
    row_scale, row_reach, col_scale, col_reach = scales(corr_ref, taper_ref, rows)
    kind, c = iota((8, LANES), 0), iota((8, LANES), 1)
    reach = jnp.where(kind % 4 < 2, LANES - c, c + 1).astype(F32)
    basis = jnp.exp(-reach / col_scale) * jnp.where(kind % 2 == 0, 1.0, reach / LANES)
    high = basis.astype(BF16)
    basis_ref[...] = jnp.where(kind < 4, high.astype(F32), basis - high.astype(F32)).astype(BF16)
    m_lane = iota((1, LANES), 1)
    cell = jnp.full((1, LANES), -1, jnp.int32)
    batches, per_batch = cells_ref.shape
    for b in range(batches):
        for n in range(per_batch):
            cell = jnp.where(m_lane == b * per_batch + n, cells_ref[b, n], cell)
    cell_row, cell_col = lax.div(cell, total_cols), lax.rem(cell, total_cols)
    row_weight = factor(cell_row - iota((rows, LANES), 0), row_scale, row_reach)
    rw_ref[...] = row_weight.astype(BF16).astype(F32)
    cw_ref[...] = factor(
        cell_col - (col * LANES + iota((LANES, LANES), 0)), col_scale, col_reach
    ).astype(BF16)


def seam(value, outer):
    group = iota(value.shape, 0)
    up = pltpu.roll(value, 1, 0)
    down = pltpu.roll(value, 7, 0)
    return jnp.where((group % 2 == 0) == (not outer), down, up)


def sweep_kernel(wells, tile_rows, total_cols, place_ref, field_ref, log_ref, basis_ref, rw_ref,
                 cw_ref, a_ref, b_ref, *refs):
    adj_refs = refs[:-5]
    mom_ref, xa_ref, xb_ref, s_ref, c_ref = refs[-5:]
    rows = field_ref.shape[0]
    seg = rows // 8
    width, parts = layout(wells)
    col = place_ref[1]
    even = lax.rem(col, 2) == 0
    a, b = a_ref[...], b_ref[...]
    sides = []
    for side in (jnp.where(even, b, a), jnp.where(even, a, b)):
        block = tile_rows // PACK
        blank = jnp.zeros((block, LANES), BF16)
        quarter = iota((block, LANES), 1) // STRIP
        second = [
            jnp.where(quarter == q, side[rows + p * block : rows + (p + 1) * block], blank)
            for p in range(rows // tile_rows) for q in range(PACK)
        ]
        sides.append((side[:rows], jnp.concatenate(second, axis=0)))
    strip = jnp.concatenate([sides[0][0], sides[1][0], sides[0][1], sides[1][1]], axis=1)
    folded = dot(fold_rows(rows), strip).astype(BF16)
    shape = (2 * LANES, parts * LANES)
    column, well = window_column(wells, shape, 1)
    src = iota(shape, 0)
    base = jnp.where(src < LANES, 0, LANES + HALO)
    slot, k = strip_slot(src % LANES, wells)
    hit = column == k + base
    k = src % STRIP
    again = (k < HALO) & (column == k + base)
    fields = field_ref[...] + dot(folded[:, : 2 * LANES], one_hot(hit & (slot == well)))
    logs = log_ref[...] + dot(folded[:, : 2 * LANES], one_hot(hit & (slot == wells)))
    logs = logs + dot(folded[:, 2 * LANES :], one_hot(again))

    cond = jnp.exp(logs)
    cond = [cond[:, i * LANES : (i + 1) * LANES] for i in range(parts)]
    lane = iota((1, LANES), 1)
    group = iota((8, LANES), 0)
    border = (group == 0) | (group == 7)
    east = [harmonic(cond[i], cond[i + 1]) for i in range(parts - 1)]
    east.append(harmonic(cond[-1], pltpu.roll(cond[0], LANES - 1, 1)))
    west = [pltpu.roll(east[-1], 1, 1)] + east[:-1]
    for i in range(parts):
        place = parts * (lane % width) + i
        column = col * LANES - HALO + place
        inside = (column >= 0) & (column < total_cols) & (place < LANES + 2 * HALO)
        here = cond[i]
        inner = harmonic(here, jnp.concatenate([here[8:], seam(here[-8:], False)], axis=0))
        first = harmonic(here[:8], seam(here[:8], True))
        outer = jnp.concatenate([jnp.where(border, here[:8], first), inner[:-8]], axis=0)
        fe = jnp.where(column < total_cols - 1, east[i], here)
        fw = jnp.where(column > 0, west[i], here)
        inverse = jnp.where(inside, 1.0 / (fe + fw + outer + inner + leakage), 0.0)
        values = [fe * inverse, fw * inverse, outer * inverse, inner * inverse]
        source = fields[:, i * LANES : (i + 1) * LANES] * inverse
        for t in range(seg):
            s_ref[(t * parts + i) * 8 : (t * parts + i + 1) * 8, :] = source[8 * t : 8 * t + 8]
            for d in range(4):
                at = ((t * parts + i) * 4 + d) * 8
                value = values[d][8 * t : 8 * t + 8]
                if t == 0 and d == 2:
                    value = jnp.where(border, 0.0, value)
                c_ref[at : at + 8, :] = value

    def load(ref, t, count=parts):
        at = t * (count * 8)
        at = at if isinstance(at, int) else pl.multiple_of(at, 8)
        return [ref[pl.ds(at + 8 * i, 8), :] for i in range(count)]

    def save(ref, t, value):
        at = t * (parts * 8)
        at = at if isinstance(at, int) else pl.multiple_of(at, 8)
        for i in range(parts):
            ref[pl.ds(at + 8 * i, 8), :] = value[i]

    def update(previous, current, following, coefs, source):
        easts = current[1:] + [pltpu.roll(current[0], LANES - 1, 1)]
        wests = [pltpu.roll(current[-1], 1, 1)] + current[:-1]
        result = []
        for i in range(parts):
            ce, cw, co, ci = coefs[4 * i : 4 * i + 4]
            result.append(
                ((source[i] + co * previous[i]) + ci * following[i])
                + (ce * easts[i] + cw * wests[i])
            )
        return result

    unroll = min(UNROLL, seg)

    def march(from_ref, to_ref):
        x1 = load(from_ref, 0)
        x0 = [seam(v, True) for v in x1]
        save(from_ref, seg, [seam(v, False) for v in load(from_ref, seg - 1)])

        def rows_of(block, carry):
            x0, x1 = carry
            for i in range(unroll):
                t = block * unroll + i
                x2 = load(from_ref, t + 1)
                save(to_ref, t, update(x0, x1, x2, load(c_ref, t, 4 * parts), load(s_ref, t)))
                x0, x1 = x1, x2
            return x0, x1

        if seg == unroll:
            rows_of(0, (x0, x1))
        else:
            lax.fori_loop(0, seg // unroll, rows_of, (x0, x1))

    march(s_ref, xa_ref)

    def more(_, carry):
        march(xa_ref, xb_ref)
        march(xb_ref, xa_ref)
        return carry

    lax.fori_loop(0, SWEEPS // 2 - 1, more, 0)

    state = jnp.concatenate(
        [
            jnp.concatenate(
                [xa_ref[(t * parts + i) * 8 : (t * parts + i + 1) * 8, :] for t in range(seg)], axis=0
            ).astype(BF16)
            for i in range(parts)
        ],
        axis=1,
    )
    shape = (parts * LANES, wells * LANES)
    column, well = window_column(wells, shape, 0)
    dst = iota(shape, 1)
    order = one_hot((column == dst % LANES + HALO) & (well == dst // LANES))
    adjoints = dot(fold_rows(rows, True), dot(state, order).astype(BF16)).astype(BF16)
    mom_ref[...] = jnp.zeros(mom_ref.shape, F32)
    span = wells * rows // 2
    both = []
    for w in range(wells):
        adjoint = adjoints[:, w * LANES : (w + 1) * LANES]
        adj_refs[w // adj_refs[0].shape[0]][w % adj_refs[0].shape[0]] = adjoint
        both.append(lax.dot_general(
            basis_ref[...], adjoint, (((1,), (1,)), ((), ())), preferred_element_type=F32
        ))
        sampled = dot(adjoint, cw_ref[...]) * rw_ref[...]
        mom_ref[w : w + 1, span : span + LANES] = jnp.sum(sampled, axis=0, keepdims=True)
    both = jnp.concatenate(both, axis=1)
    both = both[0:4] + both[4:8]
    for h in range(2):
        mom_ref[4 * h : 4 * h + 4, :span] = both[:, h * span : (h + 1) * span]


def moment(mom_ref, index, which):
    span = mom_ref.shape[2] - LANES
    return jnp.concatenate(
        [mom_ref[index, which + 4 * h : which + 4 * h + 1, :span] for h in range(2)], axis=1
    )


def factor_kernel(place_ref, corr_ref, taper_ref, mats_ref, row_ref, spread_ref):
    rows = row_ref.shape[0]
    col, taper = place_ref[1], taper_ref[1]
    row_scale, row_reach, col_scale, col_reach = scales(corr_ref, taper_ref, rows)
    kind, c = iota((16, LANES), 0), iota((16, LANES), 1)
    near = jnp.where(kind % 4 < 2, c, LANES - 1 - c).astype(F32)
    spread = jnp.exp(-near / col_scale) * jnp.where(
        kind % 2 == 0, 1.0 - near / col_reach, -LANES / col_reach
    )
    high = spread.astype(BF16).astype(F32)
    spread = jnp.where(kind < 8, high, jnp.where(kind < 12, spread - high, 0.0))
    spread_ref[...] = spread.astype(BF16)
    src, dst = iota((LANES, LANES), 0), iota((LANES, LANES), 1)
    even = lax.rem(lax.div(col, taper), 2) == 0
    shift = jnp.where(even, taper, -taper) * LANES
    for i, away in enumerate((0, shift, -shift)):
        mats_ref[i] = factor(dst - src - away, col_scale, col_reach).astype(BF16)
    offset = iota((rows, rows), 0) - iota((rows, rows), 1)
    row_ref[...] = factor(offset, row_scale, row_reach).astype(BF16)


def moment_kernel(offsets, place_ref, corr_ref, taper_ref, mom_ref, mats_ref, spread_ref, *refs):
    half = len(refs) // 2
    adj_refs, out_refs = refs[:half], refs[half:]
    col, taper = place_ref[1], taper_ref[1]
    col_scale = corr_ref[1] * BLOCK
    scale_v = jnp.ones((1, LANES), F32) * col_scale
    per, rows, _ = adj_refs[0].shape
    span = half * per * rows
    sums = [jnp.zeros((1, span), F32) for _ in range(4)]
    for index, offset in enumerate(offsets):
        if offset == 0:
            continue
        away = lax.bitwise_xor(col, offset) - col
        for side, k in ((0, -away), (1, away)):
            live = (k >= 1) & (k < taper)
            gap = jnp.maximum(k - 1, 0).astype(F32)
            gain = jnp.where(live, 1.0, 0.0) * jnp.exp(-gap * LANES / scale_v)
            gain = gain[:, :1]
            zero = moment(mom_ref, index, 2 * side)
            one = moment(mom_ref, index, 2 * side + 1)
            sums[2 * side] = sums[2 * side] + gain * zero
            sums[2 * side + 1] = sums[2 * side + 1] + gain * (gap * zero + one)
    stacked = jnp.concatenate(sums * 4, axis=0)
    kind = iota((16, span), 0)
    high = stacked.astype(BF16).astype(F32)
    stacked = jnp.where((kind >= 4) & (kind < 8), stacked - high, high).astype(BF16)
    for w in range(half * per):
        base = lax.dot_general(
            stacked[:, w * rows : (w + 1) * rows], spread_ref[...],
            (((0,), (0,)), ((), ())), preferred_element_type=F32,
        )
        out_refs[w // per][w % per] = base + dot(adj_refs[w // per][w % per], mats_ref[0])


def mix_kernel(swapped, tiles, place_ref, base_ref, mats_ref, row_ref, *refs):
    out_refs = refs[tiles:]
    wells, rows, _ = base_ref.shape
    for w in range(wells):
        mixed = base_ref[w]
        for i in range(tiles):
            mixed = mixed + dot(refs[i][w], mats_ref[1 + i])
        mixed = mixed.astype(BF16)
        if swapped:
            half = rows // 2
            other = pl.multiple_of((1 - place_ref[0]) * half, half)
            out_refs[0][w] = dot(row_ref[pl.ds(other, half), :], mixed).astype(BF16)
            out_refs[1][w] = mixed
        else:
            out_refs[0][w] = dot(row_ref[...], mixed).astype(BF16)


def keep_kernel(place_ref, mixed_ref, row_ref, out_ref):
    half = out_ref.shape[1]
    mine = pl.multiple_of(place_ref[0] * half, half)
    for w in range(mixed_ref.shape[0]):
        out_ref[w] = dot(row_ref[pl.ds(mine, half), :], mixed_ref[w]).astype(BF16)


VMEM = pl.BlockSpec(memory_space=pltpu.VMEM)
SMEM = pl.BlockSpec(memory_space=pltpu.SMEM)


def call(kernel, smem, vmem, outs, scratch=(), flops=1, whole=VMEM, limit=48 * 2**20):
    return pl.pallas_call(
        kernel,
        in_specs=[SMEM] * len(smem) + [whole] * len(vmem),
        out_specs=[VMEM] * len(outs),
        out_shape=[jax.ShapeDtypeStruct(shape, dtype) for shape, dtype in outs],
        scratch_shapes=list(scratch),
        compiler_params=pltpu.CompilerParams(vmem_limit_bytes=limit),
        cost_estimate=pl.CostEstimate(flops=flops, bytes_accessed=2**20, transcendentals=0),
    )(*smem, *vmem)


def pairs_at(count, distance, odd):
    pairs = []
    for i in range(count - distance):
        if (i // distance) % 2 == odd:
            pairs += [(i, i + distance), (i + distance, i)]
    return pairs


def exchanged(value, axis):
    return lax.ppermute(value, axis, [(0, 1), (1, 0)])


def local(log_trans, corr_len, taper_width, well_cells, obs_weight):
    tile_rows, tile_cols = log_trans.shape
    row_count, col_count = lax.axis_size("row"), lax.axis_size("col")
    total_rows, total_cols = tile_rows * row_count, tile_cols * col_count
    well_count = well_cells.shape[1]
    wells = well_count // row_count
    row, col = lax.axis_index("row"), lax.axis_index("col")
    place = jnp.stack([row, col]).astype(jnp.int32)
    own = obs_weight[0]
    swapped = row_count == 2
    tile = (wells, total_rows, tile_cols)

    if swapped:
        sent, kept = [
            lax.dynamic_slice_in_dim(own, first * wells, wells, axis=0) for first in (1 - row, row)
        ]
        (planes,) = call(
            split_kernel, (), (log_trans,), [((3, tile_rows, tile_cols), BF16)]
        )
        operands = (kept, planes, exchanged(sent, "row"), exchanged(log_trans, "row"))
    else:
        operands = (
            lax.all_to_all(own, "row", 0, 1, tiled=True),
            lax.all_gather(log_trans, "row", axis=0, tiled=True),
        )
    packed = call(
        functools.partial(pack_kernel, swapped), (place,), operands,
        [((total_rows + total_rows // PACK, LANES), BF16)] * 2,
    )
    received = [
        lax.ppermute(value, "col", pairs_at(col_count, 1, odd)) for odd, value in enumerate(packed)
    ]
    parts = layout(wells)[1]
    placed = ((total_rows, parts * LANES), F32)
    prepared = call(
        functools.partial(own_kernel, swapped, wells, total_cols),
        (place, corr_len, taper_width, well_cells), operands,
        [placed, placed, ((8, LANES), BF16), ((total_rows, LANES), F32), ((LANES, LANES), BF16)],
        [pltpu.VMEM((total_rows, (wells + 3) * LANES), BF16)],
    )
    seg = total_rows // 8
    chunks = min(CHUNKS, wells)
    piece = (wells // chunks,) + tile[1:]
    *adjoints, moments = call(
        functools.partial(sweep_kernel, wells, tile_rows if swapped else total_rows, total_cols),
        (place,), (*prepared, *received),
        [(piece, BF16)] * chunks + [((8, wells * total_rows // 2 + LANES), F32)],
        [
            pltpu.VMEM(((seg + 1) * parts * 8, LANES), F32),
            pltpu.VMEM(((seg + 1) * parts * 8, LANES), F32),
            pltpu.VMEM(((seg + 1) * parts * 8, LANES), F32),
            pltpu.VMEM((seg * parts * 32, LANES), F32),
        ],
    )

    def finish(distance, moments, *adjoints):
        borders = [pairs_at(col_count, distance, odd) for odd in range(2)]
        borders = [pairs for pairs in borders if pairs]
        tiles = [[lax.ppermute(part, "col", pairs) for pairs in borders] for part in adjoints]
        mats, row_mix, spread = call(
            factor_kernel, (place, corr_len, taper_width), (),
            [((3, LANES, LANES), BF16), ((total_rows, total_rows), BF16), ((16, LANES), BF16)],
        )
        gathered, offsets = moments[None], [0]
        steps = [1 << i for i in range(col_count.bit_length() - 1)][::-1]
        if distance == 3:
            steps[-2:] = steps[:-3:-1]
        for step in steps:
            moved = lax.ppermute(gathered, "col", [(i, i ^ step) for i in range(col_count)])
            gathered = jnp.concatenate([gathered, moved], axis=0)
            offsets = offsets + [offset ^ step for offset in offsets]
        samples = [gathered[i, :wells, -LANES:] for i in range(col_count)]
        while len(samples) > 1:
            samples = [a + b for a, b in zip(samples[::2], samples[1::2])]
        samples = samples[0][:, : 2 * well_count]
        bases = call(
            functools.partial(moment_kernel, tuple(offsets)), (place, corr_len, taper_width),
            (gathered, mats, spread, *adjoints), [(piece, F32)] * chunks,
        )
        low, front = row == 0, lax.axis_index("sect") == 0
        if swapped:
            theirs = exchanged(samples, "row")
            samples = jnp.concatenate(
                [jnp.where(low, samples, theirs), jnp.where(low, theirs, samples)], axis=0
            )
        else:
            samples = lax.all_gather(samples, "row", axis=0, tiled=True)
        theirs = exchanged(samples, "sect")
        samples = jnp.concatenate(
            [jnp.where(front, samples, theirs), jnp.where(front, theirs, samples)], axis=0
        ).T
        half = (piece[0], tile_rows, tile_cols)
        kept, others = [], []
        for base, received in zip(bases, tiles):
            fields = call(
                functools.partial(mix_kernel, swapped, len(borders)), (place,),
                (base, mats, row_mix, *received),
                [(half, BF16), (piece, BF16)] if swapped else [(piece, BF16)],
            )
            if swapped:
                others.append(exchanged(fields[0], "row"))
                fields = call(keep_kernel, (place,), (fields[1], row_mix), [(half, BF16)])
            kept.append(fields[0])
        if swapped:
            qh_fields = jnp.concatenate(
                [jnp.where(low, a, b) for a, b in zip(kept, others)]
                + [jnp.where(low, b, a) for a, b in zip(kept, others)], axis=0
            )
        else:
            qh_fields = lax.all_to_all(jnp.concatenate(kept), "row", 1, 0, tiled=True)
        return qh_fields[None], samples

    branches = [functools.partial(finish, distance) for distance in range(1, TAPER + 1)]
    return lax.switch(taper_width[1] - 1, branches, moments, *adjoints)


def solution(mesh):
    placed = (P("row", "col"), P(), P(), P(), P("sect", None, "row", "col"))
    return jax.shard_map(
        local,
        mesh=mesh,
        in_specs=placed,
        out_specs=(P("sect", None, "row", "col"), P()),
        check_vma=False,
    )
```
